1024 devices in a mesh: section: 32 (over y, z_hi, core), blk: 8 (over x), head: 4 (over z_lo).
Axes of the slice: x: 8, y: 8, z: 8 (z_hi: 2, z_lo: 4; z = z_hi * 4 + z_lo), core: 2. Of those that a mesh axis runs over, the one named last changes fastest.
Arguments:
- queries: bfloat16 [32, 2048, 2048], P('section', ('blk', 'head')), may hold values from -24 to 24
- keys_values: bfloat16 [32, 2048, 1024], P('section', ('blk', 'head')), may hold values from -8 to 8
- segment_ids: int32 [32, 2048], P('section', ('blk', 'head')), may hold values from 0 to 3, never falling along the last dimension, each value on 1 to 1536 neighbouring positions
Outputs:
- attended: bfloat16 [32, 2048, 2048], P('section', ('blk', 'head'))
The draws below stay inside these ranges and needn't reach their ends.
All inputs are finite; a program needn't handle non-finite values.
Results may differ from the reference program's by a relative error of at most 0.004.
Values may be sent and summed in bfloat16 or wider, within the bound.
No kernel may reach another device: no remote copies, remote signals or barrier semaphores. Data moves between devices by JAX's collectives and lax.ppermute only.
A program may use at most 32 MiB of HBM per device.

```python
import math
import jax
import jax.numpy as jnp
import numpy as np
from jax import lax

QUERY_HEADS = 16
KEY_VALUE_HEADS = 4
HEAD_SIZE = 128
SEQUENCE_COUNT = 32
SEQUENCE_LENGTH = 2048


def draw_keys_values(key, part):
    base_offset = jax.random.normal(jax.random.fold_in(key, 1), (SEQUENCE_COUNT, SEQUENCE_LENGTH, KEY_VALUE_HEADS, 2, HEAD_SIZE), jnp.float32)
    base_offset = jnp.clip(base_offset, -6.0, 6.0)
    return base_offset.reshape(SEQUENCE_COUNT, SEQUENCE_LENGTH, 2 * KEY_VALUE_HEADS * HEAD_SIZE).astype(jnp.bfloat16)


def draw_queries(key, part):
    base_offset = jax.random.normal(jax.random.fold_in(key, 3), (SEQUENCE_COUNT, SEQUENCE_LENGTH, QUERY_HEADS, HEAD_SIZE), jnp.float32)
    base_offset = jnp.clip(base_offset, -6.0, 6.0)
    return base_offset.reshape(SEQUENCE_COUNT, SEQUENCE_LENGTH, QUERY_HEADS * HEAD_SIZE).astype(jnp.bfloat16)


def profile(count, total, most, slope):
    portions = [(1 << 20) // math.isqrt(rank ** slope) + 1 for rank in range(2, count + 1)]
    surplus, counts = total - most - (count - 1), [1] * (count - 1)
    while surplus > 0:
        candidates = [i for i in range(count - 1) if counts[i] < most]
        whole, budget = sum([portions[i] for i in candidates]), surplus
        for i in candidates:
            extra = min(most - counts[i], max(1, budget * portions[i] // whole), surplus)
            counts[i] = counts[i] + extra
            surplus = surplus - extra
    return np.array([most] + counts)


def uneven(rng, amount, total, most, skew):
    if amount == 2:
        one = jax.random.randint(rng, (), max(1, total - most), min(most, total - 1) + 1)
        return jnp.stack([one, total - one])
    tallies = jnp.asarray(profile(amount, total, most, skew), jnp.int32)
    pairs = (amount - 1) // 2
    giver, receiver = tallies[1:1 + 2 * pairs:2], tallies[2:2 + 2 * pairs:2]
    margin = jnp.minimum(giver - 1, most - receiver)
    passed = jax.random.randint(jax.random.fold_in(rng, 1), (pairs,), 0, 1 << 20) % (margin + 1)
    tallies = tallies.at[1:1 + 2 * pairs:2].set(giver - passed).at[2:2 + 2 * pairs:2].set(receiver + passed)
    return tallies[jax.random.permutation(jax.random.fold_in(rng, 2), amount)]


def setup_inputs(seed: int = 0) -> dict:
    splits = jax.random.split(jax.random.key(seed), 4)
    queries = draw_queries(jax.random.fold_in(splits[3], 71), 0)
    keys_values = draw_keys_values(jax.random.fold_in(splits[3], 71), 0)
    segment_ids = jax.vmap(lambda own: jnp.searchsorted(jnp.cumsum(uneven(own, 4, SEQUENCE_LENGTH, SEQUENCE_LENGTH * 3 // 4, 2)), jnp.arange(SEQUENCE_LENGTH), side="right"))(jax.random.split(splits[2], SEQUENCE_COUNT)).reshape((SEQUENCE_COUNT, SEQUENCE_LENGTH)).astype(jnp.int32)
    return dict(queries=queries, keys_values=keys_values, segment_ids=segment_ids)


NEG_FILL = -1e+30

def attend_head(query_head, key_head, value_head, labels):
    token_length = query_head.shape[0]
    scores = jnp.dot(query_head, key_head.T, preferred_element_type=jnp.float32) / math.sqrt(HEAD_SIZE)
    places = jnp.arange(token_length, dtype=jnp.int32)
    allowed = (places[None, :] <= places[:, None]) & (labels[None, :] == labels[:, None])
    scores = jnp.where(allowed, scores, NEG_FILL)
    top = lax.optimization_barrier(jnp.max(scores, axis=1, keepdims=True))
    weights = jnp.where(allowed, jnp.exp(scores - top), 0.0)
    total = lax.optimization_barrier(jnp.sum(weights, axis=1, keepdims=True))
    mixed = jnp.dot(weights.astype(jnp.bfloat16), value_head, preferred_element_type=jnp.float32)
    return (mixed / total).astype(jnp.bfloat16)

def attend_sequence(inputs):
    query_rows, paired_rows, labels = inputs
    token_length = query_rows.shape[0]
    query_heads = query_rows.reshape(token_length, QUERY_HEADS, HEAD_SIZE).transpose(1, 0, 2)
    token_pairs = paired_rows.reshape(token_length, KEY_VALUE_HEADS, 2, HEAD_SIZE)
    grouped_key_heads = jnp.repeat(token_pairs[:, :, 0, :].transpose(1, 0, 2), QUERY_HEADS // KEY_VALUE_HEADS, axis=0)
    grouped_value_heads = jnp.repeat(token_pairs[:, :, 1, :].transpose(1, 0, 2), QUERY_HEADS // KEY_VALUE_HEADS, axis=0)

    def one_head(item):
        return attend_head(item[0], item[1], item[2], labels)
    mixed = lax.map(one_head, (query_heads, grouped_key_heads, grouped_value_heads))
    return mixed.transpose(1, 0, 2).reshape(token_length, QUERY_HEADS * HEAD_SIZE)

def reference(queries, keys_values, segment_ids):
    mixed = lax.map(attend_sequence, (queries, keys_values, segment_ids))
    return jnp.roll(mixed, 1, axis=0)
```

```python
import functools
import math

import jax
import jax.numpy as jnp
from jax import lax
from jax.experimental import pallas as pl
from jax.experimental.pallas import tpu as pltpu
from jax.sharding import PartitionSpec as P

HEAD_SIZE = 128
NEG_FILL = -1e30
LONGEST_SEGMENT = 1536
LABELS = 4
LABEL_ROWS = 8
NO_LABEL = 9.0


def prepare_kernel(place_ref, kv_ref, label_ref, q_ref, pair_ref, *rest, heads):
    q_refs, label_rows = rest[:-1], rest[-1]
    tokens = kv_ref.shape[0]
    kv_width = kv_ref.shape[1] // heads
    q_width = q_ref.shape[1] // heads
    label_rows[...] = jnp.full(label_rows.shape, NO_LABEL, jnp.float32)
    label_rows[0:1, 0:tokens] = label_ref[...].astype(jnp.float32)
    for which in range(heads):
        pair_ref[which, 0:tokens, :] = kv_ref[:, which * kv_width : (which + 1) * kv_width]
        pair_ref[which, tokens : tokens + LABEL_ROWS, :] = label_rows[...].astype(jnp.bfloat16)
    own = place_ref[1]
    for turn in range(heads):
        start = pl.multiple_of(lax.rem(own + turn, heads) * q_width, q_width)
        q_refs[turn][...] = q_ref[:, pl.ds(start, q_width)]


def attend_kernel(place_ref, *refs, heads, back, scale):
    q_refs = refs[:heads]
    pair_refs = refs[heads : heads + back + 1]
    out_refs = refs[heads + back + 1 : 2 * heads + back + 1]
    top_ref, total_ref, sum_ref = refs[2 * heads + back + 1 :]
    tokens = q_refs[0].shape[0]
    grouped = q_refs[0].shape[1] // HEAD_SIZE
    rows = tokens * heads
    block_index, own = place_ref[0], place_ref[1]
    first = block_index * rows
    base = jnp.maximum(block_index - back, 0) * rows

    counts = [jnp.zeros((LABEL_ROWS, HEAD_SIZE), jnp.float32) for _ in range(LABELS)]
    for distance in range(back + 1):
        valid = (block_index >= distance).astype(jnp.float32)
        for piece in range(heads):
            found = pair_refs[distance][piece, tokens : tokens + LABEL_ROWS, 0:HEAD_SIZE]
            found = found.astype(jnp.float32)
            for label in range(1, LABELS):
                counts[label] += jnp.where(found < label, valid, 0.0)
    begins = [base + jnp.sum(counts[label]).astype(jnp.int32) for label in range(1, LABELS)]

    def begin_of(position):
        found = jnp.full_like(position, base)
        for begin in begins:
            found = jnp.maximum(found, jnp.where(begin <= position, begin, base))
        return found

    earliest = base
    for begin in begins:
        earliest = jnp.maximum(earliest, jnp.where(begin <= first, begin, base))

    def keys_of(distance):
        return pair_refs[distance][:, 0:tokens, 0:HEAD_SIZE].reshape(rows, HEAD_SIZE)

    def values_of(distance):
        return pair_refs[distance][:, 0:tokens, HEAD_SIZE : 2 * HEAD_SIZE].reshape(rows, HEAD_SIZE)

    def queries_of(turn):
        return jnp.concatenate(
            [q_refs[turn][:, j * HEAD_SIZE : (j + 1) * HEAD_SIZE] for j in range(grouped)], axis=0
        )

    def positions_of(turn):
        chunk = lax.rem(own - turn + heads, heads)
        row = lax.broadcasted_iota(jnp.int32, (tokens, 1), 0)
        place = first + chunk * tokens + row
        return jnp.concatenate([place] * grouped, axis=0)

    def scores_of(turn, distance):
        scores = lax.dot_general(
            queries_of(turn),
            keys_of(distance),
            (((1,), (1,)), ((), ())),
            preferred_element_type=jnp.float32,
        )
        place = positions_of(turn)
        key_place = (block_index - distance) * rows + lax.broadcasted_iota(jnp.int32, (1, rows), 1)
        allowed = key_place >= begin_of(place)
        if distance == 0:
            allowed = allowed & (key_place <= place)
        return jnp.where(allowed, scores, NEG_FILL)

    def mixed_of(weights, distance):
        return jnp.dot(
            weights.astype(jnp.bfloat16), values_of(distance), preferred_element_type=jnp.float32
        )

    for turn in range(heads):
        scores = scores_of(turn, 0)
        top = jnp.max(scores, axis=1, keepdims=True)
        weights = jnp.exp2((scores - top) * scale)
        top_ref[turn] = top
        total_ref[turn] = jnp.sum(weights, axis=1, keepdims=True)
        sum_ref[turn] = mixed_of(weights, 0)

    for distance in range(1, back + 1):
        last = (block_index - distance) * rows + rows - 1

        @pl.when((block_index >= distance) & (last >= earliest))
        def _(distance=distance):
            for turn in range(heads):
                scores = scores_of(turn, distance)
                old = top_ref[turn]
                top = jnp.maximum(old, jnp.max(scores, axis=1, keepdims=True))
                weights = jnp.exp2((scores - top) * scale)
                factor = jnp.exp2((old - top) * scale)
                top_ref[turn] = top
                total_ref[turn] = total_ref[turn] * factor + jnp.sum(weights, axis=1, keepdims=True)
                sum_ref[turn] = sum_ref[turn] * factor + mixed_of(weights, distance)

    for turn in range(heads):
        normed = (sum_ref[turn] / total_ref[turn]).astype(jnp.bfloat16)
        for j in range(grouped):
            out_refs[turn][:, j * HEAD_SIZE : (j + 1) * HEAD_SIZE] = normed[
                j * tokens : (j + 1) * tokens
            ]


def assemble_kernel(place_ref, *refs, heads):
    pieces, out_ref = refs[:heads], refs[heads]
    width = pieces[0].shape[1]
    own = place_ref[1]
    for turn in range(heads):
        start = pl.multiple_of(lax.rem(own + turn, heads) * width, width)
        out_ref[:, pl.ds(start, width)] = pieces[turn][...]


def whole(count):
    return [pl.BlockSpec(memory_space=pltpu.VMEM)] * count


def place_spec():
    return pl.BlockSpec(memory_space=pltpu.SMEM)


def per_device(queries, keys_values, segment_ids):
    sections = lax.axis_size("section")
    blocks = lax.axis_size("blk")
    heads = lax.axis_size("head")
    tokens = queries.shape[1]
    rows = tokens * heads
    kv_width = keys_values.shape[2] // heads
    q_width = queries.shape[2] // heads
    back = min(blocks - 1, -(-LONGEST_SEGMENT // rows))
    place = jnp.stack([lax.axis_index("blk"), lax.axis_index("head")]).astype(jnp.int32)

    pair_shape = (heads, tokens + LABEL_ROWS, kv_width)
    prepared = pl.pallas_call(
        functools.partial(prepare_kernel, heads=heads),
        out_shape=[jax.ShapeDtypeStruct(pair_shape, jnp.bfloat16)]
        + [jax.ShapeDtypeStruct((tokens, q_width), jnp.bfloat16)] * heads,
        in_specs=[place_spec()] + whole(3),
        out_specs=whole(1 + heads),
        scratch_shapes=[pltpu.VMEM((LABEL_ROWS, kv_width), jnp.float32)],
        name="prepare",
    )(place, keys_values[0], segment_ids, queries[0])
    pairs, turned = prepared[0], prepared[1:]

    own_pairs = lax.all_to_all(pairs, "head", split_axis=0, concat_axis=0, tiled=True)
    earlier = [
        lax.ppermute(own_pairs, "blk", [(i, i + d) for i in range(blocks - d)])
        for d in range(1, back + 1)
    ]
    block_queries = [turned[0]] + [
        lax.ppermute(turned[t], "head", [(i, (i + t) % heads) for i in range(heads)])
        for t in range(1, heads)
    ]

    scale = math.log2(math.e) / math.sqrt(HEAD_SIZE)
    grouped = q_width // HEAD_SIZE
    attended = pl.pallas_call(
        functools.partial(attend_kernel, heads=heads, back=back, scale=scale),
        out_shape=[jax.ShapeDtypeStruct((tokens, q_width), jnp.bfloat16)] * heads,
        in_specs=[place_spec()] + whole(heads + 1 + back),
        out_specs=whole(heads),
        scratch_shapes=[
            pltpu.VMEM((heads, grouped * tokens, 1), jnp.float32),
            pltpu.VMEM((heads, grouped * tokens, 1), jnp.float32),
            pltpu.VMEM((heads, grouped * tokens, HEAD_SIZE), jnp.float32),
        ],
        compiler_params=pltpu.CompilerParams(vmem_limit_bytes=32 << 20),
        name="attend",
    )(place, *block_queries, own_pairs, *earlier)

    def index(section, block, head):
        return ((section % sections) * blocks + block) * heads + head % heads

    received = [
        lax.ppermute(
            attended[t],
            ("section", "blk", "head"),
            [
                (index(s, b, h), index(s + 1, b, h - t))
                for s in range(sections)
                for b in range(blocks)
                for h in range(heads)
            ],
        )
        for t in range(heads)
    ]
    result = pl.pallas_call(
        functools.partial(assemble_kernel, heads=heads),
        out_shape=jax.ShapeDtypeStruct(queries.shape[1:], jnp.bfloat16),
        in_specs=[place_spec()] + whole(heads),
        out_specs=pl.BlockSpec(memory_space=pltpu.VMEM),
        name="assemble",
    )(place, *received)
    return result[None]


def solution(mesh):
    return jax.shard_map(
        per_device,
        mesh=mesh,
        in_specs=(
            P("section", ("blk", "head"), None),
            P("section", ("blk", "head"), None),
            P("section", ("blk", "head")),
        ),
        out_specs=P("section", ("blk", "head"), None),
        check_vma=False,
    )
```

```python
import functools
import math

import jax
import jax.numpy as jnp
from jax import lax
from jax.experimental import pallas as pl
from jax.experimental.pallas import tpu as pltpu
from jax.sharding import PartitionSpec as P

HEAD_SIZE = 128
NEG_FILL = -1e30
LONGEST_SEGMENT = 1536
LABELS = 4
LABEL_ROWS = 8
NO_LABEL = 9.0
NEAR = 4


def prepare_kernel(kv_ref, label_ref, q_ref, out_ref, label_rows, *, heads):
    tokens = kv_ref.shape[0]
    width = kv_ref.shape[1] // heads
    q_width = q_ref.shape[1] // heads
    label_rows[...] = jnp.full(label_rows.shape, NO_LABEL, jnp.float32)
    label_rows[0:1, 0:tokens] = label_ref[...].astype(jnp.float32)
    for which in range(heads):
        out_ref[which, 0:tokens, :] = kv_ref[:, which * width : (which + 1) * width]
        for part in range(q_width // width):
            start = which * q_width + part * width
            out_ref[which, (1 + part) * tokens : (2 + part) * tokens, :] = q_ref[
                :, start : start + width
            ]
        out_ref[which, out_ref.shape[1] - LABEL_ROWS :, :] = label_rows[...].astype(jnp.bfloat16)


def pack_kernel(given_ref, out_ref, label_rows, *, tokens):
    heads = given_ref.shape[0]
    rows = heads * tokens
    keys = given_ref[:, 0:tokens, 0:HEAD_SIZE].reshape(rows, HEAD_SIZE)
    values = given_ref[:, 0:tokens, HEAD_SIZE : 2 * HEAD_SIZE].reshape(rows, HEAD_SIZE)
    out_ref[0:HEAD_SIZE, :] = values.T
    for part in range(rows // HEAD_SIZE):
        out_ref[HEAD_SIZE : 2 * HEAD_SIZE, part * HEAD_SIZE : (part + 1) * HEAD_SIZE] = keys[
            part * HEAD_SIZE : (part + 1) * HEAD_SIZE
        ]
    label_rows[...] = jnp.zeros(label_rows.shape, jnp.float32)
    found = given_ref[:, given_ref.shape[1] - LABEL_ROWS :, :].astype(jnp.float32)
    for label in range(1, LABELS):
        below = jnp.sum(jnp.where(found < label, 1.0, 0.0), axis=0)
        label_rows[label : label + 1, :] = jnp.sum(below, axis=0, keepdims=True)
    out_ref[2 * HEAD_SIZE :, :] = label_rows[...].astype(jnp.bfloat16)


def count_labels(pair_refs, distances, block_index):
    count = jnp.zeros((LABEL_ROWS, 2 * HEAD_SIZE), jnp.float32)
    for distance, ref in zip(distances, pair_refs, strict=True):
        valid = jnp.where(block_index >= distance, 1.0, 0.0)
        count += ref[2 * HEAD_SIZE :, :].astype(jnp.float32) * valid
    return [jnp.sum(count[label : label + 1]).astype(jnp.int32) for label in range(1, LABELS)]


def begin_of(position, begins, base):
    found = jnp.full_like(position, base)
    for begin in begins:
        found = jnp.maximum(found, jnp.where(begin <= position, begin, base))
    return found


def scalar_begin(position, begins, base):
    found = base
    for begin in begins:
        found = jnp.maximum(found, jnp.where(begin <= position, begin, base))
    return found


def keys_of(ref):
    held = ref[HEAD_SIZE : 2 * HEAD_SIZE, :]
    parts = held.shape[1] // HEAD_SIZE
    return jnp.concatenate(
        [held[:, part * HEAD_SIZE : (part + 1) * HEAD_SIZE] for part in range(parts)], axis=0
    )


def values_of(ref):
    return ref[0:HEAD_SIZE, :]


def queries_of(given_ref, chunk, tokens, grouped):
    parts = given_ref.shape[2] // HEAD_SIZE
    pieces = []
    for j in range(grouped):
        row, column = (1 + j // parts) * tokens, (j % parts) * HEAD_SIZE
        pieces.append(given_ref[chunk, row : row + tokens, column : column + HEAD_SIZE])
    return jnp.concatenate(pieces, axis=0)


def positions_of(first, chunk, tokens, grouped):
    lane = lax.broadcasted_iota(jnp.int32, (1, grouped * tokens), 1)
    return first + chunk * tokens + lax.rem(lane, tokens)


def scores_of(keys, queries, key_first, place, begin, causal):
    scores = lax.dot_general(
        keys, queries, (((1,), (1,)), ((), ())), preferred_element_type=jnp.float32
    )
    key_place = key_first + lax.broadcasted_iota(jnp.int32, (scores.shape[0], 1), 0)
    allowed = key_place >= begin
    if causal:
        allowed = allowed & (key_place <= place)
    return jnp.where(allowed, scores, NEG_FILL)


def fold(state, keys, values, queries, key_first, place, begin, causal, scale):
    scores = scores_of(keys, queries, key_first, place, begin, causal)
    top = jnp.max(scores, axis=0, keepdims=True)
    if state is not None:
        old, total, mixed = state
        top = jnp.maximum(old, top)
    weights = jnp.exp2((scores - top) * scale)
    added = jnp.sum(weights, axis=0, keepdims=True)
    moved = jnp.dot(values, weights.astype(jnp.bfloat16), preferred_element_type=jnp.float32)
    if state is None:
        return top, added, moved
    factor = jnp.exp2((old - top) * scale)
    return top, total * factor + added, mixed * factor + moved


def near_kernel(given_ref, *refs, tokens, grouped, near, scale):
    pair_refs = refs[:near]
    count_ref, top_ref, total_ref, mixed_ref = refs[near:]
    heads = given_ref.shape[0]
    rows = tokens * heads
    block_index, own = lax.axis_index("blk"), lax.axis_index("head")
    first = block_index * rows
    base = jnp.maximum(block_index - (near - 1), 0) * rows
    counts = count_labels(pair_refs, range(near), block_index)
    for which, count in enumerate(counts):
        count_ref[which] = count
    begins = [base + count for count in counts]
    earliest = scalar_begin(first, begins, base)

    def chunk_of(turn):
        return lax.rem(own - turn + heads, heads)

    def step(turn, distance, state, keys, values):
        chunk = chunk_of(turn)
        place = positions_of(first, chunk, tokens, grouped)
        return fold(
            state,
            keys,
            values,
            queries_of(given_ref, chunk, tokens, grouped),
            (block_index - distance) * rows,
            place,
            begin_of(place, begins, base),
            distance == 0,
            scale,
        )

    def put(turn, state):
        top_ref[turn], total_ref[turn], mixed_ref[turn] = state

    keys, values = keys_of(pair_refs[0]), values_of(pair_refs[0])
    for turn in range(heads):
        put(turn, step(turn, 0, None, keys, values))
    for distance in range(1, near):
        last = (block_index - distance) * rows + rows - 1

        @pl.when((block_index >= distance) & (last >= earliest))
        def _(distance=distance):
            keys = keys_of(pair_refs[distance])
            values = values_of(pair_refs[distance])
            for turn in range(heads):
                state = top_ref[turn], total_ref[turn], mixed_ref[turn]
                put(turn, step(turn, distance, state, keys, values))


def far_kernel(
    count_ref,
    given_ref,
    top_ref,
    total_ref,
    mixed_ref,
    *refs,
    turn,
    tokens,
    grouped,
    near,
    back,
    scale,
):
    pair_refs = refs[: back + 1 - near]
    out_ref, new_total, new_mixed, new_top = refs[back + 1 - near :]
    heads = given_ref.shape[0]
    rows = tokens * heads
    block_index, own = lax.axis_index("blk"), lax.axis_index("head")
    first = block_index * rows
    base = jnp.maximum(block_index - back, 0) * rows
    new_top[...] = top_ref[turn]
    new_total[...] = total_ref[turn]
    new_mixed[...] = mixed_ref[turn]

    @pl.when(block_index >= near)
    def _():
        counts = count_labels(pair_refs, range(near, back + 1), block_index)
        begins = [base + count + count_ref[which] for which, count in enumerate(counts)]
        earliest = scalar_begin(first, begins, base)
        chunk = lax.rem(own - turn + heads, heads)
        place = positions_of(first, chunk, tokens, grouped)
        begin = begin_of(place, begins, base)
        for distance in range(near, back + 1):
            last = (block_index - distance) * rows + rows - 1

            @pl.when((block_index >= distance) & (last >= earliest))
            def _(distance=distance):
                ref = pair_refs[distance - near]
                new_top[...], new_total[...], new_mixed[...] = fold(
                    (new_top[...], new_total[...], new_mixed[...]),
                    keys_of(ref),
                    values_of(ref),
                    queries_of(given_ref, chunk, tokens, grouped),
                    (block_index - distance) * rows,
                    place,
                    begin,
                    False,
                    scale,
                )

    normed = (new_mixed[...] / new_total[...]).T.astype(jnp.bfloat16)
    for j in range(grouped):
        out_ref[:, j * HEAD_SIZE : (j + 1) * HEAD_SIZE] = normed[j * tokens : (j + 1) * tokens]


def assemble_kernel(*refs, heads):
    pieces, out_ref, semaphores = refs[:heads], refs[heads], refs[heads + 1]
    width = pieces[0].shape[1]
    own = lax.axis_index("head")
    copies = []
    for turn in range(heads):
        start = pl.multiple_of(lax.rem(own + turn, heads) * width, width)
        copies.append(
            pltpu.make_async_copy(
                pieces[turn], out_ref.at[:, pl.ds(start, width)], semaphores.at[turn]
            )
        )
        copies[-1].start()
    for copy in copies:
        copy.wait()


def vmem(count):
    return [pl.BlockSpec(memory_space=pltpu.VMEM)] * count


def cost(tiles, rows, width):
    return pl.CostEstimate(
        flops=4 * tiles * rows * rows * width,
        bytes_accessed=tiles * rows * width * 4,
        transcendentals=tiles * rows * rows,
    )


def per_device(queries, keys_values, segment_ids):
    sections = lax.axis_size("section")
    blocks = lax.axis_size("blk")
    heads = lax.axis_size("head")
    tokens = queries.shape[1]
    rows = tokens * heads
    kv_width = keys_values.shape[2] // heads
    q_width = queries.shape[2] // heads
    grouped = q_width // HEAD_SIZE
    back = min(blocks - 1, -(-LONGEST_SEGMENT // rows))
    near = min(NEAR, back)
    scale = math.log2(math.e) / math.sqrt(HEAD_SIZE)

    parts = 1 + q_width // kv_width
    prepared = pl.pallas_call(
        functools.partial(prepare_kernel, heads=heads),
        out_shape=jax.ShapeDtypeStruct(
            (heads, parts * tokens + LABEL_ROWS, kv_width), jnp.bfloat16
        ),
        in_specs=vmem(3),
        out_specs=vmem(1)[0],
        scratch_shapes=[pltpu.VMEM((LABEL_ROWS, kv_width), jnp.float32)],
        compiler_params=pltpu.CompilerParams(vmem_limit_bytes=4 << 20),
        name="prepare",
    )(keys_values[0], segment_ids, queries[0])
    given = lax.all_to_all(prepared, "head", split_axis=0, concat_axis=0, tiled=True)
    own_pairs = pl.pallas_call(
        functools.partial(pack_kernel, tokens=tokens),
        out_shape=jax.ShapeDtypeStruct((2 * HEAD_SIZE + LABEL_ROWS, rows), jnp.bfloat16),
        in_specs=vmem(1),
        out_specs=vmem(1)[0],
        scratch_shapes=[pltpu.VMEM((LABEL_ROWS, kv_width), jnp.float32)],
        compiler_params=pltpu.CompilerParams(vmem_limit_bytes=4 << 20),
        name="pack",
    )(given)
    earlier = [
        lax.ppermute(own_pairs, "blk", [(i, i + d) for i in range(blocks - d)])
        for d in range(1, back + 1)
    ]

    lanes = grouped * tokens
    state = [
        jax.ShapeDtypeStruct((heads, 1, lanes), jnp.float32),
        jax.ShapeDtypeStruct((heads, 1, lanes), jnp.float32),
        jax.ShapeDtypeStruct((heads, HEAD_SIZE, lanes), jnp.float32),
    ]
    counts, *state = pl.pallas_call(
        functools.partial(near_kernel, tokens=tokens, grouped=grouped, near=near, scale=scale),
        out_shape=[jax.ShapeDtypeStruct((LABELS - 1,), jnp.int32)] + state,
        in_specs=vmem(1 + near),
        out_specs=[pl.BlockSpec(memory_space=pltpu.SMEM)] + vmem(3),
        compiler_params=pltpu.CompilerParams(vmem_limit_bytes=16 << 20),
        cost_estimate=cost(near * heads, rows, HEAD_SIZE),
        name="attend_near",
    )(given, own_pairs, *earlier[: near - 1])

    def index(section, block, head):
        return ((section % sections) * blocks + block) * heads + head % heads

    received = []
    for turn in range(heads):
        attended = pl.pallas_call(
            functools.partial(
                far_kernel,
                turn=turn,
                tokens=tokens,
                grouped=grouped,
                near=near,
                back=back,
                scale=scale,
            ),
            out_shape=jax.ShapeDtypeStruct((tokens, q_width), jnp.bfloat16),
            in_specs=[pl.BlockSpec(memory_space=pltpu.SMEM)] + vmem(4 + back + 1 - near),
            out_specs=vmem(1)[0],
            scratch_shapes=[
                pltpu.VMEM((1, lanes), jnp.float32),
                pltpu.VMEM((HEAD_SIZE, lanes), jnp.float32),
                pltpu.VMEM((1, lanes), jnp.float32),
            ],
            compiler_params=pltpu.CompilerParams(vmem_limit_bytes=16 << 20),
            cost_estimate=cost(back + 1 - near, rows, HEAD_SIZE),
            name="attend_far",
        )(counts, given, *state, *earlier[near - 1 :])
        route = [
            (index(s, b, h), index(s + 1, b, h - turn))
            for s in range(sections)
            for b in range(blocks)
            for h in range(heads)
        ]
        received.append(lax.ppermute(attended, ("section", "blk", "head"), route))
    result = pl.pallas_call(
        functools.partial(assemble_kernel, heads=heads),
        out_shape=jax.ShapeDtypeStruct(queries.shape[1:], jnp.bfloat16),
        in_specs=vmem(heads),
        out_specs=pl.BlockSpec(memory_space=pl.ANY),
        scratch_shapes=[pltpu.SemaphoreType.DMA((heads,))],
        compiler_params=pltpu.CompilerParams(vmem_limit_bytes=4 << 20),
        name="assemble",
    )(*received)
    return result[None]


def solution(mesh):
    return jax.shard_map(
        per_device,
        mesh=mesh,
        in_specs=(
            P("section", ("blk", "head"), None),
            P("section", ("blk", "head"), None),
            P("section", ("blk", "head")),
        ),
        out_specs=P("section", ("blk", "head"), None),
        check_vma=False,
    )
```

```python
import functools
import math

import jax
import jax.numpy as jnp
from jax import lax
from jax.experimental import pallas as pl
from jax.experimental.pallas import tpu as pltpu
from jax.sharding import PartitionSpec as P

HEAD_SIZE = 128
NEG_FILL = -1e30
LONGEST_SEGMENT = 1536
LABELS = 4
LABEL_ROWS = 8
NO_LABEL = 9.0
NEAR = 3
PREPARE_VMEM = 56 << 20
SEND_ORDER = (2, 3, 1, 0)


def prepare_kernel(
    kv_ref, label_ref, q_ref, out_ref, own_labels, label_rows, packed_rows, semaphores, *, heads
):
    tokens = kv_ref.shape[0]
    width = kv_ref.shape[1] // heads
    q_parts = q_ref.shape[1] // heads // width
    copies = []

    def start(source, target):
        copies.append(pltpu.make_async_copy(source, target, semaphores.at[len(copies)]))
        copies[-1].start()

    start(label_ref, own_labels)
    for which in range(heads):
        start(
            kv_ref.at[:, pl.ds(which * width, width)],
            out_ref.at[which, pl.ds(0, tokens), :],
        )
        for part in range(q_parts):
            start(
                q_ref.at[:, pl.ds((which * q_parts + part) * width, width)],
                out_ref.at[which, pl.ds((1 + part) * tokens, tokens), :],
            )
    copies[0].wait()
    label_rows[...] = jnp.full(label_rows.shape, NO_LABEL, jnp.float32)
    label_rows[0:1, 0:tokens] = own_labels[...].astype(jnp.float32)
    packed_rows[...] = label_rows[...].astype(jnp.bfloat16)
    for which in range(heads):
        start(packed_rows, out_ref.at[which, pl.ds(out_ref.shape[1] - LABEL_ROWS, LABEL_ROWS), :])
    for copy in copies[1:]:
        copy.wait()


def pack_kernel(given_ref, out_ref, label_rows, *, tokens):
    heads = given_ref.shape[0]
    rows = heads * tokens
    keys = given_ref[:, 0:tokens, 0:HEAD_SIZE].reshape(rows, HEAD_SIZE)
    values = given_ref[:, 0:tokens, HEAD_SIZE : 2 * HEAD_SIZE].reshape(rows, HEAD_SIZE)
    out_ref[0:HEAD_SIZE, :] = values.T
    for part in range(rows // HEAD_SIZE):
        out_ref[HEAD_SIZE : 2 * HEAD_SIZE, part * HEAD_SIZE : (part + 1) * HEAD_SIZE] = keys[
            part * HEAD_SIZE : (part + 1) * HEAD_SIZE
        ]
    label_rows[...] = jnp.zeros(label_rows.shape, jnp.float32)
    found = given_ref[:, given_ref.shape[1] - LABEL_ROWS :, :].astype(jnp.float32)
    for label in range(1, LABELS):
        below = jnp.sum(jnp.where(found < label, 1.0, 0.0), axis=0)
        label_rows[label : label + 1, :] = jnp.sum(below, axis=0, keepdims=True)
    out_ref[2 * HEAD_SIZE :, :] = label_rows[...].astype(jnp.bfloat16)


def count_labels(pair_refs, distances, block_index):
    count = jnp.zeros((LABEL_ROWS, 2 * HEAD_SIZE), jnp.float32)
    for distance, ref in zip(distances, pair_refs, strict=True):
        valid = jnp.where(block_index >= distance, 1.0, 0.0)
        count += ref[2 * HEAD_SIZE :, :].astype(jnp.float32) * valid
    return [jnp.sum(count[label : label + 1]).astype(jnp.int32) for label in range(1, LABELS)]


def begin_of(position, begins, base):
    found = jnp.full_like(position, base)
    for begin in begins:
        found = jnp.maximum(found, jnp.where(begin <= position, begin, base))
    return found


def keys_of(ref):
    held = ref[HEAD_SIZE : 2 * HEAD_SIZE, :]
    parts = held.shape[1] // HEAD_SIZE
    return jnp.concatenate(
        [held[:, part * HEAD_SIZE : (part + 1) * HEAD_SIZE] for part in range(parts)], axis=0
    )


def values_of(ref):
    return ref[0:HEAD_SIZE, :]


def queries_of(given_ref, chunk, tokens, grouped):
    parts = given_ref.shape[2] // HEAD_SIZE
    pieces = []
    for j in range(grouped):
        row, column = (1 + j // parts) * tokens, (j % parts) * HEAD_SIZE
        pieces.append(given_ref[chunk, row : row + tokens, column : column + HEAD_SIZE])
    return jnp.concatenate(pieces, axis=0)


def positions_of(first, chunk, tokens, grouped):
    lane = lax.broadcasted_iota(jnp.int32, (1, grouped * tokens), 1)
    return first + chunk * tokens + lax.rem(lane, tokens)


def fold(state, pair_refs, queries, key_first, place, begin, scale):
    keys = jnp.concatenate([keys_of(ref) for ref in pair_refs], axis=0)
    values = jnp.concatenate([values_of(ref) for ref in pair_refs], axis=1)
    scores = lax.dot_general(
        keys, queries, (((1,), (1,)), ((), ())), preferred_element_type=jnp.float32
    )
    key = lax.broadcasted_iota(jnp.int32, scores.shape, 0)
    allowed = key >= begin - key_first
    if place is not None:
        allowed = allowed & (key <= place - key_first)
    scores = jnp.where(allowed, scores, NEG_FILL)
    top = jnp.max(scores, axis=0, keepdims=True)
    if state is not None:
        old, total, mixed = state
        top = jnp.maximum(old, top)
    weights = jnp.exp2((scores - top) * scale)
    added = jnp.sum(weights, axis=0, keepdims=True)
    moved = jnp.dot(values, weights.astype(jnp.bfloat16), preferred_element_type=jnp.float32)
    if state is None:
        return top, added, moved
    factor = jnp.exp2((old - top) * scale)
    return top, total * factor + added, mixed * factor + moved


def near_kernel(given_ref, *refs, tokens, grouped, near, scale):
    pair_refs = refs[:near]
    count_ref, top_ref, total_ref, mixed_ref = refs[near:]
    heads = given_ref.shape[0]
    rows = tokens * heads
    block_index, own = lax.axis_index("blk"), lax.axis_index("head")
    first = block_index * rows
    base = jnp.maximum(block_index - (near - 1), 0) * rows
    counts = count_labels(pair_refs, range(near), block_index)
    for which, count in enumerate(counts):
        count_ref[which] = count
    begins = [base + count for count in counts]
    for turn in range(heads):
        chunk = lax.rem(own - turn + heads, heads)
        place = positions_of(first, chunk, tokens, grouped)
        top_ref[turn], total_ref[turn], mixed_ref[turn] = fold(
            None,
            pair_refs[::-1],
            queries_of(given_ref, chunk, tokens, grouped),
            first - (near - 1) * rows,
            place,
            begin_of(place, begins, base),
            scale,
        )


def far_kernel(count_ref, given_ref, top_ref, total_ref, mixed_ref, *refs, tokens, grouped, near, back, scale):
    pair_refs = refs[: back + 1 - near]
    heads = given_ref.shape[0]
    out_refs = refs[back + 1 - near : back + 1 - near + heads]
    new_total, new_mixed = refs[back + 1 - near + heads :]
    rows = tokens * heads
    block_index, own = lax.axis_index("blk"), lax.axis_index("head")
    first = block_index * rows
    base = jnp.maximum(block_index - back, 0) * rows

    @pl.when(block_index < near)
    def _():
        new_total[...] = total_ref[...]
        new_mixed[...] = mixed_ref[...]

    @pl.when(block_index >= near)
    def _():
        counts = count_labels(pair_refs, range(near, back + 1), block_index)
        begins = [base + count + count_ref[which] for which, count in enumerate(counts)]
        for turn in range(heads):
            chunk = lax.rem(own - turn + heads, heads)
            place = positions_of(first, chunk, tokens, grouped)
            _, new_total[turn], new_mixed[turn] = fold(
                (top_ref[turn], total_ref[turn], mixed_ref[turn]),
                pair_refs[::-1],
                queries_of(given_ref, chunk, tokens, grouped),
                first - back * rows,
                None,
                begin_of(place, begins, base),
                scale,
            )

    for turn in range(heads):
        normed = (new_mixed[turn] * (1.0 / new_total[turn])).astype(jnp.bfloat16).T
        for j in range(grouped):
            out_refs[turn][:, j * HEAD_SIZE : (j + 1) * HEAD_SIZE] = normed[
                j * tokens : (j + 1) * tokens
            ]


def assemble_kernel(*refs, heads):
    pieces, out_ref, semaphores = refs[:heads], refs[heads], refs[heads + 1]
    width = pieces[0].shape[1]
    own = lax.axis_index("head")
    copies = []
    for turn in range(heads):
        start = pl.multiple_of(lax.rem(own + turn, heads) * width, width)
        copies.append(
            pltpu.make_async_copy(
                pieces[turn], out_ref.at[:, pl.ds(start, width)], semaphores.at[turn]
            )
        )
        copies[-1].start()
    for copy in copies:
        copy.wait()


def vmem(count):
    return [pl.BlockSpec(memory_space=pltpu.VMEM)] * count


def cost(tiles, rows, width):
    return pl.CostEstimate(
        flops=4 * tiles * rows * rows * width,
        bytes_accessed=tiles * rows * width * 4,
        transcendentals=tiles * rows * rows,
    )


def call_near(given, pairs, tokens, grouped, near, scale):
    heads, lanes = given.shape[0], grouped * tokens
    state = [
        jax.ShapeDtypeStruct((heads, 1, lanes), jnp.float32),
        jax.ShapeDtypeStruct((heads, 1, lanes), jnp.float32),
        jax.ShapeDtypeStruct((heads, HEAD_SIZE, lanes), jnp.float32),
    ]
    counts, *state = pl.pallas_call(
        functools.partial(near_kernel, tokens=tokens, grouped=grouped, near=near, scale=scale),
        out_shape=[jax.ShapeDtypeStruct((LABELS - 1,), jnp.int32)] + state,
        in_specs=vmem(1 + near),
        out_specs=[pl.BlockSpec(memory_space=pltpu.SMEM)] + vmem(3),
        compiler_params=pltpu.CompilerParams(vmem_limit_bytes=16 << 20),
        cost_estimate=cost(near * heads, heads * tokens, HEAD_SIZE),
        name="attend_near",
    )(given, *pairs)
    return counts, state


def call_far(counts, given, state, pairs, tokens, grouped, near, back, scale):
    heads, lanes = given.shape[0], grouped * tokens
    return pl.pallas_call(
        functools.partial(
            far_kernel, tokens=tokens, grouped=grouped, near=near, back=back, scale=scale
        ),
        out_shape=[jax.ShapeDtypeStruct((tokens, grouped * HEAD_SIZE), jnp.bfloat16)] * heads,
        in_specs=[pl.BlockSpec(memory_space=pltpu.SMEM)] + vmem(4 + back + 1 - near),
        out_specs=vmem(heads),
        scratch_shapes=[
            pltpu.VMEM((heads, 1, lanes), jnp.float32),
            pltpu.VMEM((heads, HEAD_SIZE, lanes), jnp.float32),
        ],
        compiler_params=pltpu.CompilerParams(vmem_limit_bytes=16 << 20),
        cost_estimate=cost((back + 1 - near) * heads, heads * tokens, HEAD_SIZE),
        name="attend_far",
    )(counts, given, *state, *pairs)


def per_device(queries, keys_values, segment_ids):
    sections = lax.axis_size("section")
    blocks = lax.axis_size("blk")
    heads = lax.axis_size("head")
    tokens = queries.shape[1]
    rows = tokens * heads
    kv_width = keys_values.shape[2] // heads
    q_width = queries.shape[2] // heads
    grouped = q_width // HEAD_SIZE
    back = min(blocks - 1, -(-LONGEST_SEGMENT // rows))
    near = min(NEAR, back)
    scale = math.log2(math.e) / math.sqrt(HEAD_SIZE)

    parts = 1 + q_width // kv_width
    prepared = pl.pallas_call(
        functools.partial(prepare_kernel, heads=heads),
        out_shape=jax.ShapeDtypeStruct(
            (heads, parts * tokens + LABEL_ROWS, kv_width), jnp.bfloat16
        ),
        in_specs=[pl.BlockSpec(memory_space=pltpu.HBM)] * 3,
        out_specs=pl.BlockSpec(memory_space=pltpu.HBM),
        scratch_shapes=[
            pltpu.VMEM((1, tokens), jnp.int32),
            pltpu.VMEM((LABEL_ROWS, kv_width), jnp.float32),
            pltpu.VMEM((LABEL_ROWS, kv_width), jnp.bfloat16),
            pltpu.SemaphoreType.DMA((1 + heads * (parts + 1),)),
        ],
        compiler_params=pltpu.CompilerParams(vmem_limit_bytes=PREPARE_VMEM),
        name="prepare",
    )(keys_values[0], segment_ids, queries[0])
    given = lax.all_to_all(prepared, "head", split_axis=0, concat_axis=0, tiled=True)
    own_pairs = pl.pallas_call(
        functools.partial(pack_kernel, tokens=tokens),
        out_shape=jax.ShapeDtypeStruct((2 * HEAD_SIZE + LABEL_ROWS, rows), jnp.bfloat16),
        in_specs=vmem(1),
        out_specs=vmem(1)[0],
        scratch_shapes=[pltpu.VMEM((LABEL_ROWS, kv_width), jnp.float32)],
        compiler_params=pltpu.CompilerParams(vmem_limit_bytes=4 << 20),
        name="pack",
    )(given)
    earlier = [
        lax.ppermute(own_pairs, "blk", [(i, i + d) for i in range(blocks - d)])
        for d in range(1, back + 1)
    ]

    counts, state = call_near(given, [own_pairs, *earlier[: near - 1]], tokens, grouped, near, scale)

    def index(section, block, head):
        return ((section % sections) * blocks + block) * heads + head % heads

    attended = call_far(
        counts, given, state, earlier[near - 1 :], tokens, grouped, near, back, scale
    )
    received = [None] * heads
    for turn in SEND_ORDER:
        route = [
            (index(s, b, h), index(s + 1, b, h - turn))
            for s in range(sections)
            for b in range(blocks)
            for h in range(heads)
        ]
        received[turn] = lax.ppermute(attended[turn], ("section", "blk", "head"), route)
    result = pl.pallas_call(
        functools.partial(assemble_kernel, heads=heads),
        out_shape=jax.ShapeDtypeStruct(queries.shape[1:], jnp.bfloat16),
        in_specs=vmem(heads),
        out_specs=pl.BlockSpec(memory_space=pl.ANY),
        scratch_shapes=[pltpu.SemaphoreType.DMA((heads,))],
        compiler_params=pltpu.CompilerParams(vmem_limit_bytes=4 << 20),
        name="assemble",
    )(*received)
    return result[None]


def solution(mesh):
    return jax.shard_map(
        per_device,
        mesh=mesh,
        in_specs=(
            P("section", ("blk", "head"), None),
            P("section", ("blk", "head"), None),
            P("section", ("blk", "head")),
        ),
        out_specs=P("section", ("blk", "head"), None),
        check_vma=False,
    )
```

```python
import functools
import math

import jax
import jax.numpy as jnp
from jax import lax
from jax.experimental import pallas as pl
from jax.experimental.pallas import tpu as pltpu
from jax.sharding import PartitionSpec as P

HEAD_SIZE = 128
NEG_FILL = -1e30
LONGEST_SEGMENT = 1536
LABELS = 4
LABEL_ROWS = 8
NO_LABEL = 9.0
NEAR = (0, 1, 4, 5, 6)
FAR = (2, 3)
PREPARE_VMEM = 56 << 20
SEND_ORDER = (2, 3, 1, 0)


def prepare_kernel(kv_ref, label_ref, q_ref, out_ref, label_rows, *, heads):
    tokens = kv_ref.shape[0]
    width = kv_ref.shape[1] // heads
    q_width = q_ref.shape[1] // heads
    label_rows[...] = jnp.full(label_rows.shape, NO_LABEL, jnp.float32)
    label_rows[0:1, 0:tokens] = label_ref[...].astype(jnp.float32)
    for which in range(heads):
        out_ref[which, 0:tokens, :] = kv_ref[:, which * width : (which + 1) * width]
        for part in range(q_width // width):
            start = which * q_width + part * width
            out_ref[which, (1 + part) * tokens : (2 + part) * tokens, :] = q_ref[
                :, start : start + width
            ]
        out_ref[which, out_ref.shape[1] - LABEL_ROWS :, :] = label_rows[...].astype(jnp.bfloat16)


def pack_kernel(given_ref, out_ref, label_rows, *, tokens):
    heads = given_ref.shape[0]
    rows = heads * tokens
    keys = given_ref[:, 0:tokens, 0:HEAD_SIZE].reshape(rows, HEAD_SIZE)
    values = given_ref[:, 0:tokens, HEAD_SIZE : 2 * HEAD_SIZE].reshape(rows, HEAD_SIZE)
    out_ref[0:HEAD_SIZE, :] = values.T
    for part in range(rows // HEAD_SIZE):
        out_ref[HEAD_SIZE : 2 * HEAD_SIZE, part * HEAD_SIZE : (part + 1) * HEAD_SIZE] = keys[
            part * HEAD_SIZE : (part + 1) * HEAD_SIZE
        ]
    label_rows[...] = jnp.zeros(label_rows.shape, jnp.float32)
    found = given_ref[:, given_ref.shape[1] - LABEL_ROWS :, :].astype(jnp.float32)
    for label in range(1, LABELS):
        below = jnp.sum(jnp.where(found < label, 1.0, 0.0), axis=0)
        below = jnp.sum(jnp.sum(below, axis=0, keepdims=True), axis=1, keepdims=True)
        label_rows[label : label + 1, :] = jnp.broadcast_to(below, (1, rows))
    out_ref[2 * HEAD_SIZE :, :] = label_rows[...].astype(jnp.bfloat16)


def counts_of(ref):
    held = ref[2 * HEAD_SIZE :, :].astype(jnp.float32)
    return [held[label : label + 1] for label in range(1, LABELS)]


def keys_of(ref):
    held = ref[HEAD_SIZE : 2 * HEAD_SIZE, :]
    parts = held.shape[1] // HEAD_SIZE
    return jnp.concatenate(
        [held[:, part * HEAD_SIZE : (part + 1) * HEAD_SIZE] for part in range(parts)], axis=0
    )


def values_of(ref):
    return ref[0:HEAD_SIZE, :]


def queries_of(given_ref, chunk, tokens, grouped):
    parts = given_ref.shape[2] // HEAD_SIZE
    pieces = []
    for j in range(grouped):
        row, column = (1 + j // parts) * tokens, (j % parts) * HEAD_SIZE
        pieces.append(given_ref[chunk, row : row + tokens, column : column + HEAD_SIZE])
    return jnp.concatenate(pieces, axis=0)


def fold(state, distances, pair_refs, own_ref, given_ref, turn, tokens, grouped, scale):
    heads = given_ref.shape[0]
    rows, lanes = heads * tokens, grouped * tokens
    block_index, own = lax.axis_index("blk"), lax.axis_index("head")
    chunk = lax.rem(own - turn + heads, heads)
    place = chunk * tokens + lax.rem(lax.broadcasted_iota(jnp.int32, (1, lanes), 1), tokens)
    own_counts = counts_of(own_ref)
    keys = jnp.concatenate([keys_of(ref) for ref in pair_refs], axis=0)
    values = jnp.concatenate([values_of(ref) for ref in pair_refs], axis=1)
    scores = lax.dot_general(
        keys,
        queries_of(given_ref, chunk, tokens, grouped),
        (((1,), (1,)), ((), ())),
        preferred_element_type=jnp.float32,
    )
    key = lax.broadcasted_iota(jnp.int32, (rows, lanes), 0)
    masked = []
    for which, distance in enumerate(distances):
        begin = jnp.zeros((1, lanes), jnp.float32)
        for own_count, count in zip(own_counts, counts_of(pair_refs[which]), strict=True):
            inside = place.astype(jnp.float32) >= own_count
            begin = jnp.maximum(begin, jnp.where(inside, count, 0.0))
        begin = jnp.where(block_index >= distance, begin.astype(jnp.int32), rows)
        allowed = key >= begin
        if distance == 0:
            allowed = allowed & (key <= place)
        masked.append(jnp.where(allowed, scores[which * rows : (which + 1) * rows], NEG_FILL))
    scores = jnp.concatenate(masked, axis=0)
    top = jnp.max(scores, axis=0, keepdims=True)
    if state is not None:
        old, total, mixed = state
        top = jnp.maximum(old, top)
    weights = jnp.exp2((scores - top) * scale)
    added = jnp.sum(weights, axis=0, keepdims=True)
    moved = jnp.dot(values, weights.astype(jnp.bfloat16), preferred_element_type=jnp.float32)
    if state is None:
        return top, added, moved
    factor = jnp.exp2((old - top) * scale)
    return top, total * factor + added, mixed * factor + moved


def near_kernel(given_ref, *refs, distances, tokens, grouped, scale):
    pair_refs = refs[: len(distances)]
    top_ref, total_ref, mixed_ref = refs[len(distances) :]
    for turn in range(given_ref.shape[0]):
        top_ref[turn], total_ref[turn], mixed_ref[turn] = fold(
            None, distances, pair_refs, pair_refs[0], given_ref, turn, tokens, grouped, scale
        )


def far_kernel(
    given_ref, own_ref, top_ref, total_ref, mixed_ref, *refs, distances, tokens, grouped, scale
):
    heads = given_ref.shape[0]
    pair_refs = refs[: len(distances)]
    out_refs = refs[len(distances) : len(distances) + heads]
    new_total, new_mixed = refs[len(distances) + heads :]
    block_index = lax.axis_index("blk")

    @pl.when(block_index < min(distances))
    def _():
        new_total[...] = total_ref[...]
        new_mixed[...] = mixed_ref[...]

    @pl.when(block_index >= min(distances))
    def _():
        for turn in range(heads):
            _, new_total[turn], new_mixed[turn] = fold(
                (top_ref[turn], total_ref[turn], mixed_ref[turn]),
                distances,
                pair_refs,
                own_ref,
                given_ref,
                turn,
                tokens,
                grouped,
                scale,
            )

    for turn in range(heads):
        normed = (new_mixed[turn] * (1.0 / new_total[turn])).astype(jnp.bfloat16).T
        for j in range(grouped):
            out_refs[turn][:, j * HEAD_SIZE : (j + 1) * HEAD_SIZE] = normed[
                j * tokens : (j + 1) * tokens
            ]


def assemble_kernel(*refs, heads):
    pieces, out_ref, semaphores = refs[:heads], refs[heads], refs[heads + 1]
    width = pieces[0].shape[1]
    own = lax.axis_index("head")
    copies = []
    for turn in range(heads):
        start = pl.multiple_of(lax.rem(own + turn, heads) * width, width)
        copies.append(
            pltpu.make_async_copy(
                pieces[turn], out_ref.at[:, pl.ds(start, width)], semaphores.at[turn]
            )
        )
        copies[-1].start()
    for copy in copies:
        copy.wait()


def vmem(count):
    return [pl.BlockSpec(memory_space=pltpu.VMEM)] * count


def cost(tiles, rows, width):
    return pl.CostEstimate(
        flops=4 * tiles * rows * rows * width,
        bytes_accessed=tiles * rows * width * 4,
        transcendentals=tiles * rows * rows,
    )


def call_near(given, pairs, distances, tokens, grouped, scale):
    heads, lanes = given.shape[0], grouped * tokens
    return pl.pallas_call(
        functools.partial(
            near_kernel, distances=distances, tokens=tokens, grouped=grouped, scale=scale
        ),
        out_shape=[
            jax.ShapeDtypeStruct((heads, 1, lanes), jnp.float32),
            jax.ShapeDtypeStruct((heads, 1, lanes), jnp.float32),
            jax.ShapeDtypeStruct((heads, HEAD_SIZE, lanes), jnp.float32),
        ],
        in_specs=vmem(1 + len(distances)),
        out_specs=vmem(3),
        compiler_params=pltpu.CompilerParams(vmem_limit_bytes=16 << 20),
        cost_estimate=cost(len(distances) * heads, heads * tokens, HEAD_SIZE),
        name="attend_near",
    )(given, *pairs)


def call_far(given, own_pairs, state, pairs, distances, tokens, grouped, scale):
    heads, lanes = given.shape[0], grouped * tokens
    return pl.pallas_call(
        functools.partial(
            far_kernel, distances=distances, tokens=tokens, grouped=grouped, scale=scale
        ),
        out_shape=[jax.ShapeDtypeStruct((tokens, grouped * HEAD_SIZE), jnp.bfloat16)] * heads,
        in_specs=vmem(5 + len(distances)),
        out_specs=vmem(heads),
        scratch_shapes=[
            pltpu.VMEM((heads, 1, lanes), jnp.float32),
            pltpu.VMEM((heads, HEAD_SIZE, lanes), jnp.float32),
        ],
        compiler_params=pltpu.CompilerParams(vmem_limit_bytes=16 << 20),
        cost_estimate=cost(len(distances) * heads, heads * tokens, HEAD_SIZE),
        name="attend_far",
    )(given, own_pairs, *state, *pairs)


def per_device(queries, keys_values, segment_ids):
    sections = lax.axis_size("section")
    blocks = lax.axis_size("blk")
    heads = lax.axis_size("head")
    tokens = queries.shape[1]
    rows = tokens * heads
    kv_width = keys_values.shape[2] // heads
    q_width = queries.shape[2] // heads
    grouped = q_width // HEAD_SIZE
    back = min(blocks - 1, -(-LONGEST_SEGMENT // rows))
    scale = math.log2(math.e) / math.sqrt(HEAD_SIZE)

    parts = 1 + q_width // kv_width
    prepared = pl.pallas_call(
        functools.partial(prepare_kernel, heads=heads),
        out_shape=jax.ShapeDtypeStruct(
            (heads, parts * tokens + LABEL_ROWS, kv_width), jnp.bfloat16
        ),
        in_specs=vmem(3),
        out_specs=vmem(1)[0],
        scratch_shapes=[pltpu.VMEM((LABEL_ROWS, kv_width), jnp.float32)],
        compiler_params=pltpu.CompilerParams(vmem_limit_bytes=PREPARE_VMEM),
        name="prepare",
    )(keys_values[0], segment_ids, queries[0])
    given = lax.all_to_all(prepared, "head", split_axis=0, concat_axis=0, tiled=True)
    own_pairs = pl.pallas_call(
        functools.partial(pack_kernel, tokens=tokens),
        out_shape=jax.ShapeDtypeStruct((2 * HEAD_SIZE + LABEL_ROWS, rows), jnp.bfloat16),
        in_specs=vmem(1),
        out_specs=vmem(1)[0],
        scratch_shapes=[pltpu.VMEM((LABEL_ROWS, kv_width), jnp.float32)],
        compiler_params=pltpu.CompilerParams(vmem_limit_bytes=4 << 20),
        name="pack",
    )(given)
    pairs = {0: own_pairs}
    for d in [d for d in NEAR + FAR if 0 < d <= back]:
        route = [(i, i + d) for i in range(blocks - d)]
        pairs[d] = lax.ppermute(own_pairs, "blk", route)
    near = tuple(d for d in NEAR if d <= back)
    far = tuple(d for d in pairs if d not in near)
    state = call_near(given, [pairs[d] for d in near], near, tokens, grouped, scale)
    attended = call_far(
        given, own_pairs, state, [pairs[d] for d in far], far, tokens, grouped, scale
    )

    def index(section, block, head):
        return ((section % sections) * blocks + block) * heads + head % heads

    received = [None] * heads
    for turn in SEND_ORDER:
        route = [
            (index(s, b, h), index(s + 1, b, h - turn))
            for s in range(sections)
            for b in range(blocks)
            for h in range(heads)
        ]
        received[turn] = lax.ppermute(attended[turn], ("section", "blk", "head"), route)
    result = pl.pallas_call(
        functools.partial(assemble_kernel, heads=heads),
        out_shape=jax.ShapeDtypeStruct(queries.shape[1:], jnp.bfloat16),
        in_specs=vmem(heads),
        out_specs=pl.BlockSpec(memory_space=pl.ANY),
        scratch_shapes=[pltpu.SemaphoreType.DMA((heads,))],
        compiler_params=pltpu.CompilerParams(vmem_limit_bytes=4 << 20),
        name="assemble",
    )(*received)
    return result[None]


def solution(mesh):
    return jax.shard_map(
        per_device,
        mesh=mesh,
        in_specs=(
            P("section", ("blk", "head"), None),
            P("section", ("blk", "head"), None),
            P("section", ("blk", "head")),
        ),
        out_specs=P("section", ("blk", "head"), None),
        check_vma=False,
    )
```

```python
import functools
import math

import jax
import jax.numpy as jnp
from jax import lax
from jax.experimental import pallas as pl
from jax.experimental.pallas import tpu as pltpu
from jax.sharding import PartitionSpec as P

HEAD_SIZE = 128
NEG_FILL = -1e30
LONGEST_SEGMENT = 1536
LABELS = 4
LABEL_ROWS = 8
NO_LABEL = 9.0
NEAR = (0, 1, 2, 5, 6)
FAR = (3, 4)
SENT = {1: 0, 2: 0, 5: 0, 6: 0, 3: 2, 4: 2}
PREPARE_VMEM = 56 << 20
SEND_ORDER = (2, 3, 1, 0)


def prepare_kernel(kv_ref, label_ref, q_ref, out_ref, label_rows, *, heads):
    tokens = kv_ref.shape[0]
    width = kv_ref.shape[1] // heads
    q_width = q_ref.shape[1] // heads
    label_rows[...] = jnp.full(label_rows.shape, NO_LABEL, jnp.float32)
    label_rows[0:1, 0:tokens] = label_ref[...].astype(jnp.float32)
    for which in range(heads):
        out_ref[which, 0:tokens, :] = kv_ref[:, which * width : (which + 1) * width]
        for part in range(q_width // width):
            start = which * q_width + part * width
            out_ref[which, (1 + part) * tokens : (2 + part) * tokens, :] = q_ref[
                :, start : start + width
            ]
        out_ref[which, out_ref.shape[1] - LABEL_ROWS :, :] = label_rows[...].astype(jnp.bfloat16)


def pack_kernel(given_ref, out_ref, label_rows, *, tokens):
    heads = given_ref.shape[0]
    rows = heads * tokens
    keys = given_ref[:, 0:tokens, 0:HEAD_SIZE].reshape(rows, HEAD_SIZE)
    values = given_ref[:, 0:tokens, HEAD_SIZE : 2 * HEAD_SIZE].reshape(rows, HEAD_SIZE)
    out_ref[0:HEAD_SIZE, :] = values.T
    for part in range(rows // HEAD_SIZE):
        out_ref[HEAD_SIZE : 2 * HEAD_SIZE, part * HEAD_SIZE : (part + 1) * HEAD_SIZE] = keys[
            part * HEAD_SIZE : (part + 1) * HEAD_SIZE
        ]
    label_rows[...] = jnp.zeros(label_rows.shape, jnp.float32)
    found = given_ref[:, given_ref.shape[1] - LABEL_ROWS :, :].astype(jnp.float32)
    for label in range(1, LABELS):
        below = jnp.sum(jnp.where(found < label, 1.0, 0.0), axis=0)
        below = jnp.sum(jnp.sum(below, axis=0, keepdims=True), axis=1, keepdims=True)
        label_rows[label : label + 1, :] = jnp.broadcast_to(below, (1, rows))
    out_ref[2 * HEAD_SIZE :, :] = label_rows[...].astype(jnp.bfloat16)


def counts_of(ref):
    held = ref[2 * HEAD_SIZE :, :].astype(jnp.float32)
    return [held[label : label + 1] for label in range(1, LABELS)]


def keys_of(ref):
    held = ref[HEAD_SIZE : 2 * HEAD_SIZE, :]
    parts = held.shape[1] // HEAD_SIZE
    return jnp.concatenate(
        [held[:, part * HEAD_SIZE : (part + 1) * HEAD_SIZE] for part in range(parts)], axis=0
    )


def values_of(ref):
    return ref[0:HEAD_SIZE, :]


def queries_of(given_ref, chunk, tokens, grouped):
    parts = given_ref.shape[2] // HEAD_SIZE
    pieces = []
    for j in range(grouped):
        row, column = (1 + j // parts) * tokens, (j % parts) * HEAD_SIZE
        pieces.append(given_ref[chunk, row : row + tokens, column : column + HEAD_SIZE])
    return jnp.concatenate(pieces, axis=0)


def fold(state, distances, pair_refs, own_ref, given_ref, turn, tokens, grouped, scale):
    heads = given_ref.shape[0]
    rows, lanes = heads * tokens, grouped * tokens
    block_index, own = lax.axis_index("blk"), lax.axis_index("head")
    chunk = lax.rem(own - turn + heads, heads)
    place = chunk * tokens + lax.rem(lax.broadcasted_iota(jnp.int32, (1, lanes), 1), tokens)
    own_counts = counts_of(own_ref)
    keys = jnp.concatenate([keys_of(ref) for ref in pair_refs], axis=0)
    values = jnp.concatenate([values_of(ref) for ref in pair_refs], axis=1)
    scores = lax.dot_general(
        keys,
        queries_of(given_ref, chunk, tokens, grouped),
        (((1,), (1,)), ((), ())),
        preferred_element_type=jnp.float32,
    )
    key = lax.broadcasted_iota(jnp.int32, (rows, lanes), 0)
    masked = []
    for which, distance in enumerate(distances):
        begin = jnp.zeros((1, lanes), jnp.float32)
        for own_count, count in zip(own_counts, counts_of(pair_refs[which]), strict=True):
            inside = place.astype(jnp.float32) >= own_count
            begin = jnp.maximum(begin, jnp.where(inside, count, 0.0))
        begin = jnp.where(block_index >= distance, begin.astype(jnp.int32), rows)
        allowed = key >= begin
        if distance == 0:
            allowed = allowed & (key <= place)
        masked.append(jnp.where(allowed, scores[which * rows : (which + 1) * rows], NEG_FILL))
    scores = jnp.concatenate(masked, axis=0)
    top = jnp.max(scores, axis=0, keepdims=True)
    if state is not None:
        old, total, mixed = state
        top = jnp.maximum(old, top)
    weights = jnp.exp2((scores - top) * scale)
    added = jnp.sum(weights, axis=0, keepdims=True)
    moved = jnp.dot(values, weights.astype(jnp.bfloat16), preferred_element_type=jnp.float32)
    if state is None:
        return top, added, moved
    factor = jnp.exp2((old - top) * scale)
    return top, total * factor + added, mixed * factor + moved


def near_kernel(given_ref, *refs, distances, tokens, grouped, scale):
    pair_refs = refs[: len(distances)]
    top_ref, total_ref, mixed_ref = refs[len(distances) :]
    for turn in range(given_ref.shape[0]):
        top_ref[turn], total_ref[turn], mixed_ref[turn] = fold(
            None, distances, pair_refs, pair_refs[0], given_ref, turn, tokens, grouped, scale
        )


def far_kernel(
    given_ref, own_ref, top_ref, total_ref, mixed_ref, *refs, distances, tokens, grouped, scale
):
    heads = given_ref.shape[0]
    pair_refs = refs[: len(distances)]
    out_refs = refs[len(distances) : len(distances) + heads]
    new_total, new_mixed = refs[len(distances) + heads :]
    block_index = lax.axis_index("blk")

    @pl.when(block_index < min(distances))
    def _():
        new_total[...] = total_ref[...]
        new_mixed[...] = mixed_ref[...]

    @pl.when(block_index >= min(distances))
    def _():
        for turn in range(heads):
            _, new_total[turn], new_mixed[turn] = fold(
                (top_ref[turn], total_ref[turn], mixed_ref[turn]),
                distances,
                pair_refs,
                own_ref,
                given_ref,
                turn,
                tokens,
                grouped,
                scale,
            )

    for turn in range(heads):
        normed = (new_mixed[turn] * (1.0 / new_total[turn])).astype(jnp.bfloat16).T
        for j in range(grouped):
            out_refs[turn][:, j * HEAD_SIZE : (j + 1) * HEAD_SIZE] = normed[
                j * tokens : (j + 1) * tokens
            ]


def assemble_kernel(*refs, heads):
    pieces, out_ref, semaphores = refs[:heads], refs[heads], refs[heads + 1]
    width = pieces[0].shape[1]
    own = lax.axis_index("head")
    copies = []
    for turn in range(heads):
        start = pl.multiple_of(lax.rem(own + turn, heads) * width, width)
        copies.append(
            pltpu.make_async_copy(
                pieces[turn], out_ref.at[:, pl.ds(start, width)], semaphores.at[turn]
            )
        )
        copies[-1].start()
    for copy in copies:
        copy.wait()


def vmem(count):
    return [pl.BlockSpec(memory_space=pltpu.VMEM)] * count


def cost(tiles, rows, width):
    return pl.CostEstimate(
        flops=4 * tiles * rows * rows * width,
        bytes_accessed=tiles * rows * width * 4,
        transcendentals=tiles * rows * rows,
    )


def call_near(given, pairs, distances, tokens, grouped, scale):
    heads, lanes = given.shape[0], grouped * tokens
    return pl.pallas_call(
        functools.partial(
            near_kernel, distances=distances, tokens=tokens, grouped=grouped, scale=scale
        ),
        out_shape=[
            jax.ShapeDtypeStruct((heads, 1, lanes), jnp.float32),
            jax.ShapeDtypeStruct((heads, 1, lanes), jnp.float32),
            jax.ShapeDtypeStruct((heads, HEAD_SIZE, lanes), jnp.float32),
        ],
        in_specs=vmem(1 + len(distances)),
        out_specs=vmem(3),
        compiler_params=pltpu.CompilerParams(vmem_limit_bytes=16 << 20),
        cost_estimate=cost(len(distances) * heads, heads * tokens, HEAD_SIZE),
        name="attend_near",
    )(given, *pairs)


def call_far(given, own_pairs, state, pairs, distances, tokens, grouped, scale):
    heads, lanes = given.shape[0], grouped * tokens
    return pl.pallas_call(
        functools.partial(
            far_kernel, distances=distances, tokens=tokens, grouped=grouped, scale=scale
        ),
        out_shape=[jax.ShapeDtypeStruct((tokens, grouped * HEAD_SIZE), jnp.bfloat16)] * heads,
        in_specs=vmem(5 + len(distances)),
        out_specs=vmem(heads),
        scratch_shapes=[
            pltpu.VMEM((heads, 1, lanes), jnp.float32),
            pltpu.VMEM((heads, HEAD_SIZE, lanes), jnp.float32),
        ],
        compiler_params=pltpu.CompilerParams(vmem_limit_bytes=16 << 20),
        cost_estimate=cost(len(distances) * heads, heads * tokens, HEAD_SIZE),
        name="attend_far",
    )(given, own_pairs, *state, *pairs)


def per_device(queries, keys_values, segment_ids):
    sections = lax.axis_size("section")
    blocks = lax.axis_size("blk")
    heads = lax.axis_size("head")
    tokens = queries.shape[1]
    rows = tokens * heads
    kv_width = keys_values.shape[2] // heads
    q_width = queries.shape[2] // heads
    grouped = q_width // HEAD_SIZE
    back = min(blocks - 1, -(-LONGEST_SEGMENT // rows))
    scale = math.log2(math.e) / math.sqrt(HEAD_SIZE)

    parts = 1 + q_width // kv_width
    prepared = pl.pallas_call(
        functools.partial(prepare_kernel, heads=heads),
        out_shape=jax.ShapeDtypeStruct(
            (heads, parts * tokens + LABEL_ROWS, kv_width), jnp.bfloat16
        ),
        in_specs=vmem(3),
        out_specs=vmem(1)[0],
        scratch_shapes=[pltpu.VMEM((LABEL_ROWS, kv_width), jnp.float32)],
        compiler_params=pltpu.CompilerParams(vmem_limit_bytes=PREPARE_VMEM),
        name="prepare",
    )(keys_values[0], segment_ids, queries[0])
    given = lax.all_to_all(prepared, "head", split_axis=0, concat_axis=0, tiled=True)
    own_pairs = pl.pallas_call(
        functools.partial(pack_kernel, tokens=tokens),
        out_shape=jax.ShapeDtypeStruct((2 * HEAD_SIZE + LABEL_ROWS, rows), jnp.bfloat16),
        in_specs=vmem(1),
        out_specs=vmem(1)[0],
        scratch_shapes=[pltpu.VMEM((LABEL_ROWS, kv_width), jnp.float32)],
        compiler_params=pltpu.CompilerParams(vmem_limit_bytes=4 << 20),
        name="pack",
    )(given)
    pairs = {0: own_pairs}
    for d, held in SENT.items():
        if d <= back:
            route = [(i, i + d - held) for i in range(held, blocks - d + held)]
            pairs[d] = lax.ppermute(pairs[held], "blk", route)
    near = tuple(d for d in NEAR if d <= back)
    far = tuple(d for d in FAR if d <= back)
    state = call_near(given, [pairs[d] for d in near], near, tokens, grouped, scale)
    attended = call_far(
        given, own_pairs, state, [pairs[d] for d in far], far, tokens, grouped, scale
    )

    def index(section, block, head):
        return ((section % sections) * blocks + block) * heads + head % heads

    received = [None] * heads
    for turn in SEND_ORDER:
        route = [
            (index(s, b, h), index(s + 1, b, h - turn))
            for s in range(sections)
            for b in range(blocks)
            for h in range(heads)
        ]
        received[turn] = lax.ppermute(attended[turn], ("section", "blk", "head"), route)
    result = pl.pallas_call(
        functools.partial(assemble_kernel, heads=heads),
        out_shape=jax.ShapeDtypeStruct(queries.shape[1:], jnp.bfloat16),
        in_specs=vmem(heads),
        out_specs=pl.BlockSpec(memory_space=pl.ANY),
        scratch_shapes=[pltpu.SemaphoreType.DMA((heads,))],
        compiler_params=pltpu.CompilerParams(vmem_limit_bytes=4 << 20),
        name="assemble",
    )(*received)
    return result[None]


def solution(mesh):
    return jax.shard_map(
        per_device,
        mesh=mesh,
        in_specs=(
            P("section", ("blk", "head"), None),
            P("section", ("blk", "head"), None),
            P("section", ("blk", "head")),
        ),
        out_specs=P("section", ("blk", "head"), None),
        check_vma=False,
    )
```

```python
import functools
import math

import jax
import jax.numpy as jnp
from jax import lax
from jax.experimental import pallas as pl
from jax.experimental.pallas import tpu as pltpu
from jax.sharding import PartitionSpec as P

HEAD_SIZE = 128
NEG_FILL = -1e30
LONGEST_SEGMENT = 1536
LABELS = 4
LABEL_ROWS = 8
NO_LABEL = 9.0
NEAR = (0, 1, 2, 5)
FAR = (6, 3, 4)
SENT = {1: 0, 2: 0, 5: 0, 6: 0, 3: 2, 4: 2}
SEND_ORDER = (2, 3, 1, 0)


def prepare_kernel(
    kv_ref, label_ref, q_ref, out_ref, own_labels, label_rows, semaphores, *, heads
):
    tokens = kv_ref.shape[0]
    width = kv_ref.shape[1] // heads
    q_parts = q_ref.shape[1] // heads // width
    copies = []

    def start(source, target):
        copies.append(pltpu.make_async_copy(source, target, semaphores.at[len(copies)]))
        copies[-1].start()

    start(label_ref, own_labels)
    for which in range(heads):
        start(
            kv_ref.at[:, pl.ds(which * width, width)],
            out_ref.at[which, pl.ds(0, tokens), :],
        )
        for part in range(q_parts):
            start(
                q_ref.at[:, pl.ds((which * q_parts + part) * width, width)],
                out_ref.at[which, pl.ds((1 + part) * tokens, tokens), :],
            )
    label_rows[...] = jnp.full(label_rows.shape, NO_LABEL, jnp.float32)
    copies[0].wait()
    label_rows[0:1, 0:tokens] = own_labels[...].astype(jnp.float32)
    for which in range(heads):
        out_ref[which, out_ref.shape[1] - LABEL_ROWS :, :] = label_rows[...].astype(jnp.bfloat16)
    for copy in copies[1:]:
        copy.wait()


def pack_kernel(given_ref, out_ref, label_rows, *, tokens):
    heads = given_ref.shape[0]
    rows = heads * tokens
    keys = given_ref[:, 0:tokens, 0:HEAD_SIZE].reshape(rows, HEAD_SIZE)
    values = given_ref[:, 0:tokens, HEAD_SIZE : 2 * HEAD_SIZE].reshape(rows, HEAD_SIZE)
    out_ref[0:HEAD_SIZE, :] = values.T
    for part in range(rows // HEAD_SIZE):
        out_ref[HEAD_SIZE : 2 * HEAD_SIZE, part * HEAD_SIZE : (part + 1) * HEAD_SIZE] = keys[
            part * HEAD_SIZE : (part + 1) * HEAD_SIZE
        ]
    label_rows[...] = jnp.zeros(label_rows.shape, jnp.float32)
    found = given_ref[:, given_ref.shape[1] - LABEL_ROWS :, :].astype(jnp.float32)
    for label in range(1, LABELS):
        below = jnp.sum(jnp.where(found < label, 1.0, 0.0), axis=0)
        below = jnp.sum(jnp.sum(below, axis=0, keepdims=True), axis=1, keepdims=True)
        label_rows[label : label + 1, :] = jnp.broadcast_to(below, (1, rows))
    out_ref[2 * HEAD_SIZE :, :] = label_rows[...].astype(jnp.bfloat16)


def counts_of(ref):
    held = ref[2 * HEAD_SIZE :, :].astype(jnp.float32)
    return [held[label : label + 1] for label in range(1, LABELS)]


def keys_of(ref):
    held = ref[HEAD_SIZE : 2 * HEAD_SIZE, :]
    parts = held.shape[1] // HEAD_SIZE
    return jnp.concatenate(
        [held[:, part * HEAD_SIZE : (part + 1) * HEAD_SIZE] for part in range(parts)], axis=0
    )


def values_of(ref):
    return ref[0:HEAD_SIZE, :]


def queries_of(given_ref, chunk, tokens, grouped):
    parts = given_ref.shape[2] // HEAD_SIZE
    pieces = []
    for j in range(grouped):
        row, column = (1 + j // parts) * tokens, (j % parts) * HEAD_SIZE
        pieces.append(given_ref[chunk, row : row + tokens, column : column + HEAD_SIZE])
    return jnp.concatenate(pieces, axis=0)


def fold(state, distances, pair_refs, own_ref, given_ref, turn, tokens, grouped, scale):
    heads = given_ref.shape[0]
    rows, lanes = heads * tokens, grouped * tokens
    block_index, own = lax.axis_index("blk"), lax.axis_index("head")
    chunk = lax.rem(own - turn + heads, heads)
    place = chunk * tokens + lax.rem(lax.broadcasted_iota(jnp.int32, (1, lanes), 1), tokens)
    own_counts = counts_of(own_ref)
    keys = jnp.concatenate([keys_of(ref) for ref in pair_refs], axis=0)
    values = jnp.concatenate([values_of(ref) for ref in pair_refs], axis=1)
    scores = lax.dot_general(
        keys,
        queries_of(given_ref, chunk, tokens, grouped),
        (((1,), (1,)), ((), ())),
        preferred_element_type=jnp.float32,
    )
    key = lax.broadcasted_iota(jnp.int32, (rows, lanes), 0)
    masked = []
    for which, distance in enumerate(distances):
        begin = jnp.zeros((1, lanes), jnp.float32)
        for own_count, count in zip(own_counts, counts_of(pair_refs[which]), strict=True):
            inside = place.astype(jnp.float32) >= own_count
            begin = jnp.maximum(begin, jnp.where(inside, count, 0.0))
        begin = jnp.where(block_index >= distance, begin.astype(jnp.int32), rows)
        allowed = key >= begin
        if distance == 0:
            allowed = allowed & (key <= place)
        masked.append(jnp.where(allowed, scores[which * rows : (which + 1) * rows], NEG_FILL))
    scores = jnp.concatenate(masked, axis=0)
    top = jnp.max(scores, axis=0, keepdims=True)
    if state is not None:
        old, total, mixed = state
        top = jnp.maximum(old, top)
    weights = jnp.exp2((scores - top) * scale)
    added = jnp.sum(weights, axis=0, keepdims=True)
    moved = jnp.dot(values, weights.astype(jnp.bfloat16), preferred_element_type=jnp.float32)
    if state is None:
        return top, added, moved
    factor = jnp.exp2((old - top) * scale)
    return top, total * factor + added, mixed * factor + moved


def near_kernel(given_ref, *refs, distances, tokens, grouped, scale):
    pair_refs = refs[: len(distances)]
    top_ref, total_ref, mixed_ref = refs[len(distances) :]
    for turn in range(given_ref.shape[0]):
        top_ref[turn], total_ref[turn], mixed_ref[turn] = fold(
            None, distances, pair_refs, pair_refs[0], given_ref, turn, tokens, grouped, scale
        )


def far_kernel(
    given_ref, own_ref, top_ref, total_ref, mixed_ref, *refs, distances, tokens, grouped, scale
):
    heads = given_ref.shape[0]
    pair_refs = refs[: len(distances)]
    out_refs = refs[len(distances) : len(distances) + heads]
    new_total, new_mixed = refs[len(distances) + heads :]
    block_index = lax.axis_index("blk")

    @pl.when(block_index < min(distances))
    def _():
        new_total[...] = total_ref[...]
        new_mixed[...] = mixed_ref[...]

    @pl.when(block_index >= min(distances))
    def _():
        for turn in range(heads):
            _, new_total[turn], new_mixed[turn] = fold(
                (top_ref[turn], total_ref[turn], mixed_ref[turn]),
                distances,
                pair_refs,
                own_ref,
                given_ref,
                turn,
                tokens,
                grouped,
                scale,
            )

    for turn in range(heads):
        normed = (new_mixed[turn] * (1.0 / new_total[turn])).astype(jnp.bfloat16).T
        for j in range(grouped):
            out_refs[turn][:, j * HEAD_SIZE : (j + 1) * HEAD_SIZE] = normed[
                j * tokens : (j + 1) * tokens
            ]


def assemble_kernel(*refs, heads):
    pieces, out_ref, semaphores = refs[:heads], refs[heads], refs[heads + 1]
    width = pieces[0].shape[1]
    own = lax.axis_index("head")
    copies = []
    for turn in range(heads):
        start = pl.multiple_of(lax.rem(own + turn, heads) * width, width)
        copies.append(
            pltpu.make_async_copy(
                pieces[turn], out_ref.at[:, pl.ds(start, width)], semaphores.at[turn]
            )
        )
        copies[-1].start()
    for copy in copies:
        copy.wait()


def vmem(count):
    return [pl.BlockSpec(memory_space=pltpu.VMEM)] * count


def cost(tiles, rows, width):
    return pl.CostEstimate(
        flops=4 * tiles * rows * rows * width,
        bytes_accessed=tiles * rows * width * 4,
        transcendentals=tiles * rows * rows,
    )


def call_near(given, pairs, distances, tokens, grouped, scale):
    heads, lanes = given.shape[0], grouped * tokens
    return pl.pallas_call(
        functools.partial(
            near_kernel, distances=distances, tokens=tokens, grouped=grouped, scale=scale
        ),
        out_shape=[
            jax.ShapeDtypeStruct((heads, 1, lanes), jnp.float32),
            jax.ShapeDtypeStruct((heads, 1, lanes), jnp.float32),
            jax.ShapeDtypeStruct((heads, HEAD_SIZE, lanes), jnp.float32),
        ],
        in_specs=vmem(1 + len(distances)),
        out_specs=vmem(3),
        compiler_params=pltpu.CompilerParams(vmem_limit_bytes=16 << 20),
        cost_estimate=cost(len(distances) * heads, heads * tokens, HEAD_SIZE),
        name="attend_near",
    )(given, *pairs)


def call_far(given, own_pairs, state, pairs, distances, tokens, grouped, scale):
    heads, lanes = given.shape[0], grouped * tokens
    return pl.pallas_call(
        functools.partial(
            far_kernel, distances=distances, tokens=tokens, grouped=grouped, scale=scale
        ),
        out_shape=[jax.ShapeDtypeStruct((tokens, grouped * HEAD_SIZE), jnp.bfloat16)] * heads,
        in_specs=vmem(5 + len(distances)),
        out_specs=vmem(heads),
        scratch_shapes=[
            pltpu.VMEM((heads, 1, lanes), jnp.float32),
            pltpu.VMEM((heads, HEAD_SIZE, lanes), jnp.float32),
        ],
        compiler_params=pltpu.CompilerParams(vmem_limit_bytes=16 << 20),
        cost_estimate=cost(len(distances) * heads, heads * tokens, HEAD_SIZE),
        name="attend_far",
    )(given, own_pairs, *state, *pairs)


def per_device(queries, keys_values, segment_ids):
    sections = lax.axis_size("section")
    blocks = lax.axis_size("blk")
    heads = lax.axis_size("head")
    tokens = queries.shape[1]
    rows = tokens * heads
    kv_width = keys_values.shape[2] // heads
    q_width = queries.shape[2] // heads
    grouped = q_width // HEAD_SIZE
    back = min(blocks - 1, -(-LONGEST_SEGMENT // rows))
    scale = math.log2(math.e) / math.sqrt(HEAD_SIZE)

    parts = 1 + q_width // kv_width
    prepared = pl.pallas_call(
        functools.partial(prepare_kernel, heads=heads),
        out_shape=jax.ShapeDtypeStruct(
            (heads, parts * tokens + LABEL_ROWS, kv_width), jnp.bfloat16
        ),
        in_specs=[pl.BlockSpec(memory_space=pltpu.HBM)] * 3,
        out_specs=vmem(1)[0],
        scratch_shapes=[
            pltpu.VMEM((1, tokens), jnp.int32),
            pltpu.VMEM((LABEL_ROWS, kv_width), jnp.float32),
            pltpu.SemaphoreType.DMA((1 + heads * parts,)),
        ],
        compiler_params=pltpu.CompilerParams(vmem_limit_bytes=4 << 20),
        name="prepare",
    )(
        pltpu.with_memory_space_constraint(keys_values[0], pltpu.HBM),
        pltpu.with_memory_space_constraint(segment_ids, pltpu.HBM),
        pltpu.with_memory_space_constraint(queries[0], pltpu.HBM),
    )
    given = lax.all_to_all(prepared, "head", split_axis=0, concat_axis=0, tiled=True)
    own_pairs = pl.pallas_call(
        functools.partial(pack_kernel, tokens=tokens),
        out_shape=jax.ShapeDtypeStruct((2 * HEAD_SIZE + LABEL_ROWS, rows), jnp.bfloat16),
        in_specs=vmem(1),
        out_specs=vmem(1)[0],
        scratch_shapes=[pltpu.VMEM((LABEL_ROWS, kv_width), jnp.float32)],
        compiler_params=pltpu.CompilerParams(vmem_limit_bytes=4 << 20),
        name="pack",
    )(given)
    pairs = {0: own_pairs}
    for d, held in SENT.items():
        if d <= back:
            route = [(i, i + d - held) for i in range(held, blocks - d + held)]
            pairs[d] = lax.ppermute(pairs[held], "blk", route)
    near = tuple(d for d in NEAR if d <= back)
    far = tuple(d for d in FAR if d <= back)
    state = call_near(given, [pairs[d] for d in near], near, tokens, grouped, scale)
    attended = call_far(
        given, own_pairs, state, [pairs[d] for d in far], far, tokens, grouped, scale
    )

    def index(section, block, head):
        return ((section % sections) * blocks + block) * heads + head % heads

    received = [None] * heads
    for turn in SEND_ORDER:
        route = [
            (index(s, b, h), index(s + 1, b, h - turn))
            for s in range(sections)
            for b in range(blocks)
            for h in range(heads)
        ]
        received[turn] = lax.ppermute(attended[turn], ("section", "blk", "head"), route)
    result = pl.pallas_call(
        functools.partial(assemble_kernel, heads=heads),
        out_shape=jax.ShapeDtypeStruct(queries.shape[1:], jnp.bfloat16),
        in_specs=vmem(heads),
        out_specs=pl.BlockSpec(memory_space=pl.ANY),
        scratch_shapes=[pltpu.SemaphoreType.DMA((heads,))],
        compiler_params=pltpu.CompilerParams(vmem_limit_bytes=4 << 20),
        name="assemble",
    )(*received)
    return result[None]


def solution(mesh):
    return jax.shard_map(
        per_device,
        mesh=mesh,
        in_specs=(
            P("section", ("blk", "head"), None),
            P("section", ("blk", "head"), None),
            P("section", ("blk", "head")),
        ),
        out_specs=P("section", ("blk", "head"), None),
        check_vma=False,
    )
```

```python
import functools
import math

import jax
import jax.numpy as jnp
from jax import lax
from jax.experimental import pallas as pl
from jax.experimental.pallas import tpu as pltpu
from jax.sharding import PartitionSpec as P

HEAD_SIZE = 128
NEG_FILL = -1e30
LONGEST_SEGMENT = 1536
LABELS = 4
LABEL_ROWS = 8
NO_LABEL = 9.0
NEAR = (0, 2, 5, 1)
FAR = (6, 4, 3)
SENT = {2: 0, 5: 0, 6: 0, 1: 0, 4: 2, 3: 2}


def prepare_kernel(
    kv_ref, label_ref, q_ref, out_ref, own_labels, label_rows, semaphores, *, heads
):
    tokens = kv_ref.shape[0]
    width = kv_ref.shape[1] // heads
    q_parts = q_ref.shape[1] // heads // width
    copies = []

    def start(source, target):
        copies.append(pltpu.make_async_copy(source, target, semaphores.at[len(copies)]))
        copies[-1].start()

    start(label_ref, own_labels)
    for which in range(heads):
        start(
            kv_ref.at[:, pl.ds(which * width, width)],
            out_ref.at[which, pl.ds(0, tokens), :],
        )
        for part in range(q_parts):
            start(
                q_ref.at[:, pl.ds((which * q_parts + part) * width, width)],
                out_ref.at[which, pl.ds((1 + part) * tokens, tokens), :],
            )
    label_rows[...] = jnp.full(label_rows.shape, NO_LABEL, jnp.float32)
    copies[0].wait()
    label_rows[0:1, 0:tokens] = own_labels[...].astype(jnp.float32)
    for which in range(heads):
        out_ref[which, out_ref.shape[1] - LABEL_ROWS :, :] = label_rows[...].astype(jnp.bfloat16)
    for copy in copies[1:]:
        copy.wait()


def pack_kernel(given_ref, out_ref, label_rows, *, tokens):
    heads = given_ref.shape[0]
    rows = heads * tokens
    keys = given_ref[:, 0:tokens, 0:HEAD_SIZE].reshape(rows, HEAD_SIZE)
    values = given_ref[:, 0:tokens, HEAD_SIZE : 2 * HEAD_SIZE].reshape(rows, HEAD_SIZE)
    out_ref[0:HEAD_SIZE, :] = values.T
    for part in range(rows // HEAD_SIZE):
        out_ref[HEAD_SIZE : 2 * HEAD_SIZE, part * HEAD_SIZE : (part + 1) * HEAD_SIZE] = keys[
            part * HEAD_SIZE : (part + 1) * HEAD_SIZE
        ]
    label_rows[...] = jnp.zeros(label_rows.shape, jnp.float32)
    found = given_ref[:, given_ref.shape[1] - LABEL_ROWS :, :].astype(jnp.float32)
    for label in range(1, LABELS):
        below = jnp.sum(jnp.where(found < label, 1.0, 0.0), axis=0)
        below = jnp.sum(jnp.sum(below, axis=0, keepdims=True), axis=1, keepdims=True)
        label_rows[label : label + 1, :] = jnp.broadcast_to(below, (1, rows))
    out_ref[2 * HEAD_SIZE :, :] = label_rows[...].astype(jnp.bfloat16)


def counts_of(ref):
    held = ref[2 * HEAD_SIZE :, :].astype(jnp.float32)
    return [held[label : label + 1] for label in range(1, LABELS)]


def keys_of(ref):
    held = ref[HEAD_SIZE : 2 * HEAD_SIZE, :]
    parts = held.shape[1] // HEAD_SIZE
    return jnp.concatenate(
        [held[:, part * HEAD_SIZE : (part + 1) * HEAD_SIZE] for part in range(parts)], axis=0
    )


def values_of(ref):
    return ref[0:HEAD_SIZE, :]


def queries_of(given_ref, chunk, tokens, grouped):
    parts = given_ref.shape[2] // HEAD_SIZE
    pieces = []
    for j in range(grouped):
        row, column = (1 + j // parts) * tokens, (j % parts) * HEAD_SIZE
        pieces.append(given_ref[chunk, row : row + tokens, column : column + HEAD_SIZE])
    return jnp.concatenate(pieces, axis=0)


def fold(state, distances, pair_refs, own_ref, given_ref, turn, tokens, grouped, scale):
    heads = given_ref.shape[0]
    rows, lanes = heads * tokens, grouped * tokens
    block_index, own = lax.axis_index("blk"), lax.axis_index("head")
    chunk = lax.rem(own - turn + heads, heads)
    place = chunk * tokens + lax.rem(lax.broadcasted_iota(jnp.int32, (1, lanes), 1), tokens)
    own_counts = counts_of(own_ref)
    keys = jnp.concatenate([keys_of(ref) for ref in pair_refs], axis=0)
    values = jnp.concatenate([values_of(ref) for ref in pair_refs], axis=1)
    scores = lax.dot_general(
        keys,
        queries_of(given_ref, chunk, tokens, grouped),
        (((1,), (1,)), ((), ())),
        preferred_element_type=jnp.float32,
    )
    key = lax.broadcasted_iota(jnp.int32, (rows, lanes), 0)
    masked = []
    for which, distance in enumerate(distances):
        begin = jnp.zeros((1, lanes), jnp.float32)
        for own_count, count in zip(own_counts, counts_of(pair_refs[which]), strict=True):
            inside = place.astype(jnp.float32) >= own_count
            begin = jnp.maximum(begin, jnp.where(inside, count, 0.0))
        begin = jnp.where(block_index >= distance, begin.astype(jnp.int32), rows)
        allowed = key >= begin
        if distance == 0:
            allowed = allowed & (key <= place)
        masked.append(jnp.where(allowed, scores[which * rows : (which + 1) * rows], NEG_FILL))
    scores = jnp.concatenate(masked, axis=0)
    top = jnp.max(scores, axis=0, keepdims=True)
    if state is not None:
        old, total, mixed = state
        top = jnp.maximum(old, top)
    weights = jnp.exp2((scores - top) * scale)
    added = jnp.sum(weights, axis=0, keepdims=True)
    moved = jnp.dot(values, weights.astype(jnp.bfloat16), preferred_element_type=jnp.float32)
    if state is None:
        return top, added, moved
    factor = jnp.exp2((old - top) * scale)
    return top, total * factor + added, mixed * factor + moved


def near_kernel(given_ref, *refs, distances, tokens, grouped, scale):
    pair_refs = refs[: len(distances)]
    top_ref, total_ref, mixed_ref = refs[len(distances) :]
    for turn in range(given_ref.shape[0]):
        top_ref[turn], total_ref[turn], mixed_ref[turn] = fold(
            None, distances, pair_refs, pair_refs[0], given_ref, turn, tokens, grouped, scale
        )


def far_kernel(
    given_ref, own_ref, top_ref, total_ref, mixed_ref, *refs, distances, tokens, grouped, scale
):
    heads = given_ref.shape[0]
    pair_refs = refs[: len(distances)]
    out_refs = refs[len(distances) : len(distances) + heads]
    new_total, new_mixed = refs[len(distances) + heads :]
    block_index = lax.axis_index("blk")

    @pl.when(block_index < min(distances))
    def _():
        new_total[...] = total_ref[...]
        new_mixed[...] = mixed_ref[...]

    @pl.when(block_index >= min(distances))
    def _():
        for turn in range(heads):
            _, new_total[turn], new_mixed[turn] = fold(
                (top_ref[turn], total_ref[turn], mixed_ref[turn]),
                distances,
                pair_refs,
                own_ref,
                given_ref,
                turn,
                tokens,
                grouped,
                scale,
            )

    for turn in range(heads):
        normed = (new_mixed[turn] * (1.0 / new_total[turn])).astype(jnp.bfloat16).T
        for j in range(grouped):
            out_refs[turn][:, j * HEAD_SIZE : (j + 1) * HEAD_SIZE] = normed[
                j * tokens : (j + 1) * tokens
            ]


def assemble_kernel(*refs, heads):
    pieces, out_ref, semaphores = refs[:heads], refs[heads], refs[heads + 1]
    width = pieces[0].shape[1]
    own = lax.axis_index("head")
    copies = []
    for turn in range(heads):
        start = pl.multiple_of(lax.rem(own + turn, heads) * width, width)
        copies.append(
            pltpu.make_async_copy(
                pieces[turn], out_ref.at[:, pl.ds(start, width)], semaphores.at[turn]
            )
        )
        copies[-1].start()
    for copy in copies:
        copy.wait()


def vmem(count):
    return [pl.BlockSpec(memory_space=pltpu.VMEM)] * count


def cost(tiles, rows, width):
    return pl.CostEstimate(
        flops=4 * tiles * rows * rows * width,
        bytes_accessed=tiles * rows * width * 4,
        transcendentals=tiles * rows * rows,
    )


def call_near(given, pairs, distances, tokens, grouped, scale):
    heads, lanes = given.shape[0], grouped * tokens
    return pl.pallas_call(
        functools.partial(
            near_kernel, distances=distances, tokens=tokens, grouped=grouped, scale=scale
        ),
        out_shape=[
            jax.ShapeDtypeStruct((heads, 1, lanes), jnp.float32),
            jax.ShapeDtypeStruct((heads, 1, lanes), jnp.float32),
            jax.ShapeDtypeStruct((heads, HEAD_SIZE, lanes), jnp.float32),
        ],
        in_specs=vmem(1 + len(distances)),
        out_specs=vmem(3),
        compiler_params=pltpu.CompilerParams(vmem_limit_bytes=16 << 20),
        cost_estimate=cost(len(distances) * heads, heads * tokens, HEAD_SIZE),
        name="attend_near",
    )(given, *pairs)


def call_far(given, own_pairs, state, pairs, distances, tokens, grouped, scale):
    heads, lanes = given.shape[0], grouped * tokens
    return pl.pallas_call(
        functools.partial(
            far_kernel, distances=distances, tokens=tokens, grouped=grouped, scale=scale
        ),
        out_shape=[jax.ShapeDtypeStruct((tokens, grouped * HEAD_SIZE), jnp.bfloat16)] * heads,
        in_specs=vmem(5 + len(distances)),
        out_specs=vmem(heads),
        scratch_shapes=[
            pltpu.VMEM((heads, 1, lanes), jnp.float32),
            pltpu.VMEM((heads, HEAD_SIZE, lanes), jnp.float32),
        ],
        compiler_params=pltpu.CompilerParams(vmem_limit_bytes=16 << 20),
        cost_estimate=cost(len(distances) * heads, heads * tokens, HEAD_SIZE),
        name="attend_far",
    )(given, own_pairs, *state, *pairs)


def per_device(queries, keys_values, segment_ids):
    sections = lax.axis_size("section")
    blocks = lax.axis_size("blk")
    heads = lax.axis_size("head")
    tokens = queries.shape[1]
    rows = tokens * heads
    kv_width = keys_values.shape[2] // heads
    q_width = queries.shape[2] // heads
    grouped = q_width // HEAD_SIZE
    back = min(blocks - 1, -(-LONGEST_SEGMENT // rows))
    scale = math.log2(math.e) / math.sqrt(HEAD_SIZE)

    parts = 1 + q_width // kv_width
    prepared = pl.pallas_call(
        functools.partial(prepare_kernel, heads=heads),
        out_shape=jax.ShapeDtypeStruct(
            (heads, parts * tokens + LABEL_ROWS, kv_width), jnp.bfloat16
        ),
        in_specs=[pl.BlockSpec(memory_space=pltpu.HBM)] * 3,
        out_specs=vmem(1)[0],
        scratch_shapes=[
            pltpu.VMEM((1, tokens), jnp.int32),
            pltpu.VMEM((LABEL_ROWS, kv_width), jnp.float32),
            pltpu.SemaphoreType.DMA((1 + heads * parts,)),
        ],
        compiler_params=pltpu.CompilerParams(vmem_limit_bytes=4 << 20),
        name="prepare",
    )(
        pltpu.with_memory_space_constraint(keys_values[0], pltpu.HBM),
        pltpu.with_memory_space_constraint(segment_ids, pltpu.HBM),
        pltpu.with_memory_space_constraint(queries[0], pltpu.HBM),
    )
    given = lax.all_to_all(prepared, "head", split_axis=0, concat_axis=0, tiled=True)
    own_pairs = pl.pallas_call(
        functools.partial(pack_kernel, tokens=tokens),
        out_shape=jax.ShapeDtypeStruct((2 * HEAD_SIZE + LABEL_ROWS, rows), jnp.bfloat16),
        in_specs=vmem(1),
        out_specs=vmem(1)[0],
        scratch_shapes=[pltpu.VMEM((LABEL_ROWS, kv_width), jnp.float32)],
        compiler_params=pltpu.CompilerParams(vmem_limit_bytes=4 << 20),
        name="pack",
    )(given)
    pairs = {0: own_pairs}
    for d, held in SENT.items():
        if d <= back:
            route = [(i, i + d - held) for i in range(held, blocks - d + held)]
            pairs[d] = lax.ppermute(pairs[held], "blk", route)
    near = tuple(d for d in NEAR if d <= back)
    far = tuple(d for d in FAR if d <= back)
    state = call_near(given, [pairs[d] for d in near], near, tokens, grouped, scale)
    attended = call_far(
        given, own_pairs, state, [pairs[d] for d in far], far, tokens, grouped, scale
    )

    def index(section, block, head):
        return ((section % sections) * blocks + block) * heads + head % heads

    received = [None] * heads
    for turn in range(heads):
        route = [
            (index(s, b, h), index(s + 1, b, h - turn))
            for s in range(sections)
            for b in range(blocks)
            for h in range(heads)
        ]
        received[turn] = lax.ppermute(attended[turn], ("section", "blk", "head"), route)
    result = pl.pallas_call(
        functools.partial(assemble_kernel, heads=heads),
        out_shape=jax.ShapeDtypeStruct(queries.shape[1:], jnp.bfloat16),
        in_specs=vmem(heads),
        out_specs=pl.BlockSpec(memory_space=pl.ANY),
        scratch_shapes=[pltpu.SemaphoreType.DMA((heads,))],
        compiler_params=pltpu.CompilerParams(vmem_limit_bytes=4 << 20),
        name="assemble",
    )(*received)
    return result[None]


def solution(mesh):
    return jax.shard_map(
        per_device,
        mesh=mesh,
        in_specs=(
            P("section", ("blk", "head"), None),
            P("section", ("blk", "head"), None),
            P("section", ("blk", "head")),
        ),
        out_specs=P("section", ("blk", "head"), None),
        check_vma=False,
    )
```

```python
import functools
import math

import jax
import jax.numpy as jnp
from jax import lax
from jax.experimental import pallas as pl
from jax.experimental.pallas import tpu as pltpu
from jax.sharding import PartitionSpec as P

HEAD_SIZE = 128
NEG_FILL = -1e30
LONGEST_SEGMENT = 1536
LABELS = 4
LABEL_ROWS = 8
NO_LABEL = 9.0
SHIFTS = (0, 1, 3, 2)
NEAR = (0, 2, 5, 1)
FAR = (6, 4, 3)
SENT = {2: 0, 5: 0, 6: 0, 1: 0, 4: 2, 3: 2}


def prepare_kernel(
    kv_ref, label_ref, q_ref, out_ref, own_labels, label_rows, semaphores, *, heads
):
    tokens = kv_ref.shape[0]
    width = kv_ref.shape[1] // heads
    q_parts = q_ref.shape[1] // heads // width
    copies = []

    def start(source, target):
        copies.append(pltpu.make_async_copy(source, target, semaphores.at[len(copies)]))
        copies[-1].start()

    start(label_ref, own_labels)
    for which in range(heads):
        start(
            kv_ref.at[:, pl.ds(which * width, width)],
            out_ref.at[which, pl.ds(0, tokens), :],
        )
        for part in range(q_parts):
            start(
                q_ref.at[:, pl.ds((which * q_parts + part) * width, width)],
                out_ref.at[which, pl.ds((1 + part) * tokens, tokens), :],
            )
    label_rows[...] = jnp.full(label_rows.shape, NO_LABEL, jnp.float32)
    copies[0].wait()
    label_rows[0:1, 0:tokens] = own_labels[...].astype(jnp.float32)
    for which in range(heads):
        out_ref[which, out_ref.shape[1] - LABEL_ROWS :, :] = label_rows[...].astype(jnp.bfloat16)
    for copy in copies[1:]:
        copy.wait()


def pack_kernel(given_ref, out_ref, label_rows, *, tokens):
    heads = given_ref.shape[0]
    rows = heads * tokens
    keys = given_ref[:, 0:tokens, 0:HEAD_SIZE].reshape(rows, HEAD_SIZE)
    values = given_ref[:, 0:tokens, HEAD_SIZE : 2 * HEAD_SIZE].reshape(rows, HEAD_SIZE)
    out_ref[0:HEAD_SIZE, :] = values.T
    for part in range(rows // HEAD_SIZE):
        out_ref[HEAD_SIZE : 2 * HEAD_SIZE, part * HEAD_SIZE : (part + 1) * HEAD_SIZE] = keys[
            part * HEAD_SIZE : (part + 1) * HEAD_SIZE
        ]
    label_rows[...] = jnp.zeros(label_rows.shape, jnp.float32)
    found = given_ref[:, given_ref.shape[1] - LABEL_ROWS :, :].astype(jnp.float32)
    for label in range(1, LABELS):
        below = jnp.sum(jnp.where(found < label, 1.0, 0.0), axis=0)
        below = jnp.sum(jnp.sum(below, axis=0, keepdims=True), axis=1, keepdims=True)
        label_rows[label : label + 1, :] = jnp.broadcast_to(below, (1, rows))
    out_ref[2 * HEAD_SIZE :, :] = label_rows[...].astype(jnp.bfloat16)


def counts_of(ref):
    held = ref[2 * HEAD_SIZE :, :].astype(jnp.float32)
    return [held[label : label + 1] for label in range(1, LABELS)]


def keys_of(ref):
    held = ref[HEAD_SIZE : 2 * HEAD_SIZE, :]
    parts = held.shape[1] // HEAD_SIZE
    return jnp.concatenate(
        [held[:, part * HEAD_SIZE : (part + 1) * HEAD_SIZE] for part in range(parts)], axis=0
    )


def values_of(ref):
    return ref[0:HEAD_SIZE, :]


def queries_of(given_ref, chunk, tokens, grouped):
    parts = given_ref.shape[2] // HEAD_SIZE
    pieces = []
    for j in range(grouped):
        row, column = (1 + j // parts) * tokens, (j % parts) * HEAD_SIZE
        pieces.append(given_ref[chunk, row : row + tokens, column : column + HEAD_SIZE])
    return jnp.concatenate(pieces, axis=0)


def fold(state, distances, pair_refs, own_ref, given_ref, turn, tokens, grouped, scale):
    heads = given_ref.shape[0]
    rows, lanes = heads * tokens, grouped * tokens
    block_index, own = lax.axis_index("blk"), lax.axis_index("head")
    chunk = lax.rem(own - SHIFTS[turn] + heads, heads)
    place = chunk * tokens + lax.rem(lax.broadcasted_iota(jnp.int32, (1, lanes), 1), tokens)
    own_counts = counts_of(own_ref)
    keys = jnp.concatenate([keys_of(ref) for ref in pair_refs], axis=0)
    values = jnp.concatenate([values_of(ref) for ref in pair_refs], axis=1)
    scores = lax.dot_general(
        keys,
        queries_of(given_ref, chunk, tokens, grouped),
        (((1,), (1,)), ((), ())),
        preferred_element_type=jnp.float32,
    )
    key = lax.broadcasted_iota(jnp.int32, (rows, lanes), 0)
    masked = []
    for which, distance in enumerate(distances):
        begin = jnp.zeros((1, lanes), jnp.float32)
        for own_count, count in zip(own_counts, counts_of(pair_refs[which]), strict=True):
            inside = place.astype(jnp.float32) >= own_count
            begin = jnp.maximum(begin, jnp.where(inside, count, 0.0))
        begin = jnp.where(block_index >= distance, begin.astype(jnp.int32), rows)
        allowed = key >= begin
        if distance == 0:
            allowed = allowed & (key <= place)
        masked.append(jnp.where(allowed, scores[which * rows : (which + 1) * rows], NEG_FILL))
    scores = jnp.concatenate(masked, axis=0)
    top = jnp.max(scores, axis=0, keepdims=True)
    if state is not None:
        old, total, mixed = state
        top = jnp.maximum(old, top)
    weights = jnp.exp2((scores - top) * scale)
    added = jnp.sum(weights, axis=0, keepdims=True)
    moved = jnp.dot(values, weights.astype(jnp.bfloat16), preferred_element_type=jnp.float32)
    if state is None:
        return top, added, moved
    factor = jnp.exp2((old - top) * scale)
    return top, total * factor + added, mixed * factor + moved


def near_kernel(given_ref, *refs, distances, tokens, grouped, scale):
    pair_refs = refs[: len(distances)]
    top_ref, total_ref, mixed_ref = refs[len(distances) :]
    for turn in range(given_ref.shape[0]):
        top_ref[turn], total_ref[turn], mixed_ref[turn] = fold(
            None, distances, pair_refs, pair_refs[0], given_ref, turn, tokens, grouped, scale
        )


def far_kernel(
    given_ref, own_ref, top_ref, total_ref, mixed_ref, *refs, distances, tokens, grouped, scale
):
    heads = given_ref.shape[0]
    pair_refs = refs[: len(distances)]
    out_refs = refs[len(distances) : len(distances) + heads]
    new_total, new_mixed = refs[len(distances) + heads :]
    block_index = lax.axis_index("blk")

    @pl.when(block_index < min(distances))
    def _():
        new_total[...] = total_ref[...]
        new_mixed[...] = mixed_ref[...]

    @pl.when(block_index >= min(distances))
    def _():
        for turn in range(heads):
            _, new_total[turn], new_mixed[turn] = fold(
                (top_ref[turn], total_ref[turn], mixed_ref[turn]),
                distances,
                pair_refs,
                own_ref,
                given_ref,
                turn,
                tokens,
                grouped,
                scale,
            )

    for turn in range(heads):
        normed = (new_mixed[turn] * (1.0 / new_total[turn])).astype(jnp.bfloat16).T
        for j in range(grouped):
            out_refs[turn][:, j * HEAD_SIZE : (j + 1) * HEAD_SIZE] = normed[
                j * tokens : (j + 1) * tokens
            ]


def assemble_kernel(*refs, heads):
    pieces, out_ref, semaphores = refs[:heads], refs[heads], refs[heads + 1]
    width = pieces[0].shape[1]
    own = lax.axis_index("head")
    copies = []
    for turn in range(heads):
        start = pl.multiple_of(lax.rem(own + SHIFTS[turn], heads) * width, width)
        copies.append(
            pltpu.make_async_copy(
                pieces[turn], out_ref.at[:, pl.ds(start, width)], semaphores.at[turn]
            )
        )
        copies[-1].start()
    for copy in copies:
        copy.wait()


def vmem(count):
    return [pl.BlockSpec(memory_space=pltpu.VMEM)] * count


def cost(tiles, rows, width):
    return pl.CostEstimate(
        flops=4 * tiles * rows * rows * width,
        bytes_accessed=tiles * rows * width * 4,
        transcendentals=tiles * rows * rows,
    )


def call_near(given, pairs, distances, tokens, grouped, scale):
    heads, lanes = given.shape[0], grouped * tokens
    return pl.pallas_call(
        functools.partial(
            near_kernel, distances=distances, tokens=tokens, grouped=grouped, scale=scale
        ),
        out_shape=[
            jax.ShapeDtypeStruct((heads, 1, lanes), jnp.float32),
            jax.ShapeDtypeStruct((heads, 1, lanes), jnp.float32),
            jax.ShapeDtypeStruct((heads, HEAD_SIZE, lanes), jnp.float32),
        ],
        in_specs=vmem(1 + len(distances)),
        out_specs=vmem(3),
        compiler_params=pltpu.CompilerParams(vmem_limit_bytes=16 << 20),
        cost_estimate=cost(len(distances) * heads, heads * tokens, HEAD_SIZE),
        name="attend_near",
    )(given, *pairs)


def call_far(given, own_pairs, state, pairs, distances, tokens, grouped, scale):
    heads, lanes = given.shape[0], grouped * tokens
    return pl.pallas_call(
        functools.partial(
            far_kernel, distances=distances, tokens=tokens, grouped=grouped, scale=scale
        ),
        out_shape=[jax.ShapeDtypeStruct((tokens, grouped * HEAD_SIZE), jnp.bfloat16)] * heads,
        in_specs=vmem(5 + len(distances)),
        out_specs=vmem(heads),
        scratch_shapes=[
            pltpu.VMEM((heads, 1, lanes), jnp.float32),
            pltpu.VMEM((heads, HEAD_SIZE, lanes), jnp.float32),
        ],
        compiler_params=pltpu.CompilerParams(vmem_limit_bytes=16 << 20),
        cost_estimate=cost(len(distances) * heads, heads * tokens, HEAD_SIZE),
        name="attend_far",
    )(given, own_pairs, *state, *pairs)


def per_device(queries, keys_values, segment_ids):
    sections = lax.axis_size("section")
    blocks = lax.axis_size("blk")
    heads = lax.axis_size("head")
    tokens = queries.shape[1]
    rows = tokens * heads
    kv_width = keys_values.shape[2] // heads
    q_width = queries.shape[2] // heads
    grouped = q_width // HEAD_SIZE
    back = min(blocks - 1, -(-LONGEST_SEGMENT // rows))
    scale = math.log2(math.e) / math.sqrt(HEAD_SIZE)

    parts = 1 + q_width // kv_width
    prepared = pl.pallas_call(
        functools.partial(prepare_kernel, heads=heads),
        out_shape=jax.ShapeDtypeStruct(
            (heads, parts * tokens + LABEL_ROWS, kv_width), jnp.bfloat16
        ),
        in_specs=[pl.BlockSpec(memory_space=pltpu.HBM)] * 3,
        out_specs=vmem(1)[0],
        scratch_shapes=[
            pltpu.VMEM((1, tokens), jnp.int32),
            pltpu.VMEM((LABEL_ROWS, kv_width), jnp.float32),
            pltpu.SemaphoreType.DMA((1 + heads * parts,)),
        ],
        compiler_params=pltpu.CompilerParams(vmem_limit_bytes=4 << 20),
        name="prepare",
    )(
        pltpu.with_memory_space_constraint(keys_values[0], pltpu.HBM),
        pltpu.with_memory_space_constraint(segment_ids, pltpu.HBM),
        pltpu.with_memory_space_constraint(queries[0], pltpu.HBM),
    )
    given = lax.all_to_all(prepared, "head", split_axis=0, concat_axis=0, tiled=True)
    own_pairs = pl.pallas_call(
        functools.partial(pack_kernel, tokens=tokens),
        out_shape=jax.ShapeDtypeStruct((2 * HEAD_SIZE + LABEL_ROWS, rows), jnp.bfloat16),
        in_specs=vmem(1),
        out_specs=vmem(1)[0],
        scratch_shapes=[pltpu.VMEM((LABEL_ROWS, kv_width), jnp.float32)],
        compiler_params=pltpu.CompilerParams(vmem_limit_bytes=4 << 20),
        name="pack",
    )(given)
    pairs = {0: own_pairs}
    for d, held in SENT.items():
        if d <= back:
            route = [(i, i + d - held) for i in range(held, blocks - d + held)]
            pairs[d] = lax.ppermute(pairs[held], "blk", route)
    near = tuple(d for d in NEAR if d <= back)
    far = tuple(d for d in FAR if d <= back)
    state = call_near(given, [pairs[d] for d in near], near, tokens, grouped, scale)
    attended = call_far(
        given, own_pairs, state, [pairs[d] for d in far], far, tokens, grouped, scale
    )

    def index(section, block, head):
        return ((section % sections) * blocks + block) * heads + head % heads

    received = [None] * heads
    for turn in range(heads):
        route = [
            (index(s, b, h), index(s + 1, b, h - SHIFTS[turn]))
            for s in range(sections)
            for b in range(blocks)
            for h in range(heads)
        ]
        received[turn] = lax.ppermute(attended[turn], ("section", "blk", "head"), route)
    result = pl.pallas_call(
        functools.partial(assemble_kernel, heads=heads),
        out_shape=jax.ShapeDtypeStruct(queries.shape[1:], jnp.bfloat16),
        in_specs=vmem(heads),
        out_specs=pl.BlockSpec(memory_space=pl.ANY),
        scratch_shapes=[pltpu.SemaphoreType.DMA((heads,))],
        compiler_params=pltpu.CompilerParams(vmem_limit_bytes=4 << 20),
        name="assemble",
    )(*received)
    return result[None]


def solution(mesh):
    return jax.shard_map(
        per_device,
        mesh=mesh,
        in_specs=(
            P("section", ("blk", "head"), None),
            P("section", ("blk", "head"), None),
            P("section", ("blk", "head")),
        ),
        out_specs=P("section", ("blk", "head"), None),
        check_vma=False,
    )
```

```python
import functools
import math

import jax
import jax.numpy as jnp
from jax import lax
from jax.experimental import pallas as pl
from jax.experimental.pallas import tpu as pltpu
from jax.sharding import PartitionSpec as P

HEAD_SIZE = 128
NEG_FILL = -1e30
LONGEST_SEGMENT = 1536
LABELS = 4
LABEL_ROWS = 8
NO_LABEL = 9.0
NEAR = (0, 2, 5, 1)
FAR = (6, 4, 3)
SENT = {2: 0, 5: 0, 6: 0, 1: 0, 4: 2, 3: 2}


def prepare_kernel(
    kv_ref, label_ref, q_ref, out_ref, own_labels, label_rows, semaphores, *, heads
):
    tokens = kv_ref.shape[0]
    width = kv_ref.shape[1] // heads
    q_parts = q_ref.shape[1] // heads // width
    copies = []

    def start(source, target):
        copies.append(pltpu.make_async_copy(source, target, semaphores.at[len(copies)]))
        copies[-1].start()

    start(label_ref, own_labels)
    for which in range(heads):
        start(
            kv_ref.at[:, pl.ds(which * width, width)],
            out_ref.at[which, pl.ds(0, tokens), :],
        )
        for part in range(q_parts):
            start(
                q_ref.at[:, pl.ds((which * q_parts + part) * width, width)],
                out_ref.at[which, pl.ds((1 + part) * tokens, tokens), :],
            )
    label_rows[...] = jnp.full(label_rows.shape, NO_LABEL, jnp.float32)
    copies[0].wait()
    label_rows[0:1, 0:tokens] = own_labels[...].astype(jnp.float32)
    for which in range(heads):
        out_ref[which, out_ref.shape[1] - LABEL_ROWS :, :] = label_rows[...].astype(jnp.bfloat16)
    for copy in copies[1:]:
        copy.wait()


def pack_kernel(given_ref, out_ref, label_rows, *, tokens):
    heads = given_ref.shape[0]
    rows = heads * tokens
    keys = given_ref[:, 0:tokens, 0:HEAD_SIZE].reshape(rows, HEAD_SIZE)
    values = given_ref[:, 0:tokens, HEAD_SIZE : 2 * HEAD_SIZE].reshape(rows, HEAD_SIZE)
    out_ref[0:HEAD_SIZE, :] = values.T
    for part in range(rows // HEAD_SIZE):
        out_ref[HEAD_SIZE : 2 * HEAD_SIZE, part * HEAD_SIZE : (part + 1) * HEAD_SIZE] = keys[
            part * HEAD_SIZE : (part + 1) * HEAD_SIZE
        ]
    label_rows[...] = jnp.zeros(label_rows.shape, jnp.float32)
    found = given_ref[:, given_ref.shape[1] - LABEL_ROWS :, :].astype(jnp.float32)
    for label in range(1, LABELS):
        below = jnp.sum(jnp.where(found < label, 1.0, 0.0), axis=0)
        below = jnp.sum(jnp.sum(below, axis=0, keepdims=True), axis=1, keepdims=True)
        label_rows[label : label + 1, :] = jnp.broadcast_to(below, (1, rows))
    out_ref[2 * HEAD_SIZE :, :] = label_rows[...].astype(jnp.bfloat16)


def counts_of(ref):
    held = ref[2 * HEAD_SIZE :, :].astype(jnp.float32)
    return [held[label : label + 1] for label in range(1, LABELS)]


def keys_of(ref):
    held = ref[HEAD_SIZE : 2 * HEAD_SIZE, :]
    parts = held.shape[1] // HEAD_SIZE
    return jnp.concatenate(
        [held[:, part * HEAD_SIZE : (part + 1) * HEAD_SIZE] for part in range(parts)], axis=0
    )


def values_of(ref):
    return ref[0:HEAD_SIZE, :]


def queries_of(given_ref, chunk, tokens, grouped):
    parts = given_ref.shape[2] // HEAD_SIZE
    pieces = []
    for j in range(grouped):
        row, column = (1 + j // parts) * tokens, (j % parts) * HEAD_SIZE
        pieces.append(given_ref[chunk, row : row + tokens, column : column + HEAD_SIZE])
    return jnp.concatenate(pieces, axis=0)


def fold(state, distances, pair_refs, own_ref, given_ref, turn, tokens, grouped, scale):
    heads = given_ref.shape[0]
    rows, lanes = heads * tokens, grouped * tokens
    block_index, own = lax.axis_index("blk"), lax.axis_index("head")
    chunk = lax.rem(own - turn + heads, heads)
    place = chunk * tokens + lax.rem(lax.broadcasted_iota(jnp.int32, (1, lanes), 1), tokens)
    own_counts = counts_of(own_ref)
    keys = jnp.concatenate([keys_of(ref) for ref in pair_refs], axis=0)
    values = jnp.concatenate([values_of(ref) for ref in pair_refs], axis=1)
    scores = lax.dot_general(
        keys,
        queries_of(given_ref, chunk, tokens, grouped),
        (((1,), (1,)), ((), ())),
        preferred_element_type=jnp.float32,
    )
    key = lax.broadcasted_iota(jnp.int32, (rows, lanes), 0)
    masked = []
    for which, distance in enumerate(distances):
        begin = jnp.zeros((1, lanes), jnp.float32)
        for own_count, count in zip(own_counts, counts_of(pair_refs[which]), strict=True):
            inside = place.astype(jnp.float32) >= own_count
            begin = jnp.maximum(begin, jnp.where(inside, count, 0.0))
        begin = jnp.where(block_index >= distance, begin.astype(jnp.int32), rows)
        allowed = key >= begin
        if distance == 0:
            allowed = allowed & (key <= place)
        masked.append(jnp.where(allowed, scores[which * rows : (which + 1) * rows], NEG_FILL))
    scores = jnp.concatenate(masked, axis=0)
    top = jnp.max(scores, axis=0, keepdims=True)
    if state is not None:
        old, total, mixed = state
        top = jnp.maximum(old, top)
    weights = jnp.exp2((scores - top) * scale)
    added = jnp.sum(weights, axis=0, keepdims=True)
    moved = jnp.dot(values, weights.astype(jnp.bfloat16), preferred_element_type=jnp.float32)
    if state is None:
        return top, added, moved
    factor = jnp.exp2((old - top) * scale)
    return top, total * factor + added, mixed * factor + moved


def near_kernel(given_ref, *refs, distances, tokens, grouped, scale):
    pair_refs = refs[: len(distances)]
    top_ref, total_ref, mixed_ref = refs[len(distances) :]
    for turn in range(given_ref.shape[0]):
        top_ref[turn], total_ref[turn], mixed_ref[turn] = fold(
            None, distances, pair_refs, pair_refs[0], given_ref, turn, tokens, grouped, scale
        )


def far_kernel(
    given_ref, own_ref, top_ref, total_ref, mixed_ref, *refs, distances, tokens, grouped, scale
):
    heads = given_ref.shape[0]
    pair_refs = refs[: len(distances)]
    out_refs = refs[len(distances) : len(distances) + heads]
    new_total, new_mixed = refs[len(distances) + heads :]
    block_index = lax.axis_index("blk")

    @pl.when(block_index < min(distances))
    def _():
        new_total[...] = total_ref[...]
        new_mixed[...] = mixed_ref[...]

    levels = sorted(distances) + [lax.axis_size("blk")]
    for level, above in zip(levels[:-1], levels[1:], strict=True):
        taken = [which for which, d in enumerate(distances) if d <= level]

        @pl.when((block_index >= level) & (block_index < above))
        def _(taken=taken):
            for turn in range(heads):
                _, new_total[turn], new_mixed[turn] = fold(
                    (top_ref[turn], total_ref[turn], mixed_ref[turn]),
                    [distances[which] for which in taken],
                    [pair_refs[which] for which in taken],
                    own_ref,
                    given_ref,
                    turn,
                    tokens,
                    grouped,
                    scale,
                )

    for turn in range(heads):
        normed = (new_mixed[turn] * (1.0 / new_total[turn])).astype(jnp.bfloat16).T
        for j in range(grouped):
            out_refs[turn][:, j * HEAD_SIZE : (j + 1) * HEAD_SIZE] = normed[
                j * tokens : (j + 1) * tokens
            ]


def assemble_kernel(*refs, heads):
    pieces, out_ref, semaphores = refs[:heads], refs[heads], refs[heads + 1]
    width = pieces[0].shape[1]
    own = lax.axis_index("head")
    copies = []
    for turn in range(heads):
        start = pl.multiple_of(lax.rem(own + turn, heads) * width, width)
        copies.append(
            pltpu.make_async_copy(
                pieces[turn], out_ref.at[:, pl.ds(start, width)], semaphores.at[turn]
            )
        )
        copies[-1].start()
    for copy in copies:
        copy.wait()


def vmem(count):
    return [pl.BlockSpec(memory_space=pltpu.VMEM)] * count


def cost(tiles, rows, width):
    return pl.CostEstimate(
        flops=4 * tiles * rows * rows * width,
        bytes_accessed=tiles * rows * width * 4,
        transcendentals=tiles * rows * rows,
    )


def call_near(given, pairs, distances, tokens, grouped, scale):
    heads, lanes = given.shape[0], grouped * tokens
    return pl.pallas_call(
        functools.partial(
            near_kernel, distances=distances, tokens=tokens, grouped=grouped, scale=scale
        ),
        out_shape=[
            jax.ShapeDtypeStruct((heads, 1, lanes), jnp.float32),
            jax.ShapeDtypeStruct((heads, 1, lanes), jnp.float32),
            jax.ShapeDtypeStruct((heads, HEAD_SIZE, lanes), jnp.float32),
        ],
        in_specs=vmem(1 + len(distances)),
        out_specs=vmem(3),
        compiler_params=pltpu.CompilerParams(vmem_limit_bytes=16 << 20),
        cost_estimate=cost(len(distances) * heads, heads * tokens, HEAD_SIZE),
        name="attend_near",
    )(given, *pairs)


def call_far(given, own_pairs, state, pairs, distances, tokens, grouped, scale):
    heads, lanes = given.shape[0], grouped * tokens
    return pl.pallas_call(
        functools.partial(
            far_kernel, distances=distances, tokens=tokens, grouped=grouped, scale=scale
        ),
        out_shape=[jax.ShapeDtypeStruct((tokens, grouped * HEAD_SIZE), jnp.bfloat16)] * heads,
        in_specs=vmem(5 + len(distances)),
        out_specs=vmem(heads),
        scratch_shapes=[
            pltpu.VMEM((heads, 1, lanes), jnp.float32),
            pltpu.VMEM((heads, HEAD_SIZE, lanes), jnp.float32),
        ],
        compiler_params=pltpu.CompilerParams(vmem_limit_bytes=16 << 20),
        cost_estimate=cost(len(distances) * heads, heads * tokens, HEAD_SIZE),
        name="attend_far",
    )(given, own_pairs, *state, *pairs)


def per_device(queries, keys_values, segment_ids):
    sections = lax.axis_size("section")
    blocks = lax.axis_size("blk")
    heads = lax.axis_size("head")
    tokens = queries.shape[1]
    rows = tokens * heads
    kv_width = keys_values.shape[2] // heads
    q_width = queries.shape[2] // heads
    grouped = q_width // HEAD_SIZE
    back = min(blocks - 1, -(-LONGEST_SEGMENT // rows))
    scale = math.log2(math.e) / math.sqrt(HEAD_SIZE)

    parts = 1 + q_width // kv_width
    prepared = pl.pallas_call(
        functools.partial(prepare_kernel, heads=heads),
        out_shape=jax.ShapeDtypeStruct(
            (heads, parts * tokens + LABEL_ROWS, kv_width), jnp.bfloat16
        ),
        in_specs=[pl.BlockSpec(memory_space=pltpu.HBM)] * 3,
        out_specs=vmem(1)[0],
        scratch_shapes=[
            pltpu.VMEM((1, tokens), jnp.int32),
            pltpu.VMEM((LABEL_ROWS, kv_width), jnp.float32),
            pltpu.SemaphoreType.DMA((1 + heads * parts,)),
        ],
        compiler_params=pltpu.CompilerParams(vmem_limit_bytes=4 << 20),
        name="prepare",
    )(
        pltpu.with_memory_space_constraint(keys_values[0], pltpu.HBM),
        pltpu.with_memory_space_constraint(segment_ids, pltpu.HBM),
        pltpu.with_memory_space_constraint(queries[0], pltpu.HBM),
    )
    given = lax.all_to_all(prepared, "head", split_axis=0, concat_axis=0, tiled=True)
    own_pairs = pl.pallas_call(
        functools.partial(pack_kernel, tokens=tokens),
        out_shape=jax.ShapeDtypeStruct((2 * HEAD_SIZE + LABEL_ROWS, rows), jnp.bfloat16),
        in_specs=vmem(1),
        out_specs=vmem(1)[0],
        scratch_shapes=[pltpu.VMEM((LABEL_ROWS, kv_width), jnp.float32)],
        compiler_params=pltpu.CompilerParams(vmem_limit_bytes=4 << 20),
        name="pack",
    )(given)
    pairs = {0: own_pairs}
    for d, held in SENT.items():
        if d <= back:
            route = [(i, i + d - held) for i in range(held, blocks - d + held)]
            pairs[d] = lax.ppermute(pairs[held], "blk", route)
    near = tuple(d for d in NEAR if d <= back)
    far = tuple(d for d in FAR if d <= back)
    state = call_near(given, [pairs[d] for d in near], near, tokens, grouped, scale)
    attended = call_far(
        given, own_pairs, state, [pairs[d] for d in far], far, tokens, grouped, scale
    )

    def index(section, block, head):
        return ((section % sections) * blocks + block) * heads + head % heads

    received = [None] * heads
    for turn in range(heads):
        route = [
            (index(s, b, h), index(s + 1, b, h - turn))
            for s in range(sections)
            for b in range(blocks)
            for h in range(heads)
        ]
        received[turn] = lax.ppermute(attended[turn], ("section", "blk", "head"), route)
    result = pl.pallas_call(
        functools.partial(assemble_kernel, heads=heads),
        out_shape=jax.ShapeDtypeStruct(queries.shape[1:], jnp.bfloat16),
        in_specs=vmem(heads),
        out_specs=pl.BlockSpec(memory_space=pl.ANY),
        scratch_shapes=[pltpu.SemaphoreType.DMA((heads,))],
        compiler_params=pltpu.CompilerParams(vmem_limit_bytes=4 << 20),
        name="assemble",
    )(*received)
    return result[None]


def solution(mesh):
    return jax.shard_map(
        per_device,
        mesh=mesh,
        in_specs=(
            P("section", ("blk", "head"), None),
            P("section", ("blk", "head"), None),
            P("section", ("blk", "head")),
        ),
        out_specs=P("section", ("blk", "head"), None),
        check_vma=False,
    )
```

```python
import functools
import math

import jax
import jax.numpy as jnp
from jax import lax
from jax.experimental import pallas as pl
from jax.experimental.pallas import tpu as pltpu
from jax.sharding import PartitionSpec as P

HEAD_SIZE = 128
NEG_FILL = -1e30
LONGEST_SEGMENT = 1536
LABELS = 4
LABEL_ROWS = 8
NO_LABEL = 9.0
NEAR = (0, 2, 5, 1)
FAR = (6, 4, 3)
SENT = {2: 0, 5: 0, 6: 0, 1: 0, 4: 2, 3: 2}


def prepare_kernel(
    kv_ref, label_ref, q_ref, out_ref, own_labels, label_rows, semaphores, *, heads
):
    tokens = kv_ref.shape[0]
    width = kv_ref.shape[1] // heads
    q_parts = q_ref.shape[1] // heads // width
    copies = []

    def start(source, target):
        copies.append(pltpu.make_async_copy(source, target, semaphores.at[len(copies)]))
        copies[-1].start()

    start(label_ref, own_labels)
    for which in range(heads):
        start(
            kv_ref.at[:, pl.ds(which * width, width)],
            out_ref.at[which, pl.ds(0, tokens), :],
        )
        for part in range(q_parts):
            start(
                q_ref.at[:, pl.ds((which * q_parts + part) * width, width)],
                out_ref.at[which, pl.ds((1 + part) * tokens, tokens), :],
            )
    label_rows[...] = jnp.full(label_rows.shape, NO_LABEL, jnp.float32)
    copies[0].wait()
    label_rows[0:1, 0:tokens] = own_labels[...].astype(jnp.float32)
    for which in range(heads):
        out_ref[which, out_ref.shape[1] - LABEL_ROWS :, :] = label_rows[...].astype(jnp.bfloat16)
    for copy in copies[1:]:
        copy.wait()


def pack_kernel(given_ref, out_ref, label_rows, *, tokens):
    heads = given_ref.shape[0]
    rows = heads * tokens
    keys = given_ref[:, 0:tokens, 0:HEAD_SIZE].reshape(rows, HEAD_SIZE)
    values = given_ref[:, 0:tokens, HEAD_SIZE : 2 * HEAD_SIZE].reshape(rows, HEAD_SIZE)
    out_ref[0:HEAD_SIZE, :] = values.T
    for part in range(rows // HEAD_SIZE):
        out_ref[HEAD_SIZE : 2 * HEAD_SIZE, part * HEAD_SIZE : (part + 1) * HEAD_SIZE] = keys[
            part * HEAD_SIZE : (part + 1) * HEAD_SIZE
        ]
    label_rows[...] = jnp.zeros(label_rows.shape, jnp.float32)
    found = given_ref[:, given_ref.shape[1] - LABEL_ROWS :, :].astype(jnp.float32)
    for label in range(1, LABELS):
        below = jnp.sum(jnp.where(found < label, 1.0, 0.0), axis=0)
        below = jnp.sum(jnp.sum(below, axis=0, keepdims=True), axis=1, keepdims=True)
        label_rows[label : label + 1, :] = jnp.broadcast_to(below, (1, rows))
    out_ref[2 * HEAD_SIZE :, :] = label_rows[...].astype(jnp.bfloat16)


def counts_of(ref):
    held = ref[2 * HEAD_SIZE :, :].astype(jnp.float32)
    return [held[label : label + 1] for label in range(1, LABELS)]


def keys_of(ref):
    held = ref[HEAD_SIZE : 2 * HEAD_SIZE, :]
    parts = held.shape[1] // HEAD_SIZE
    return jnp.concatenate(
        [held[:, part * HEAD_SIZE : (part + 1) * HEAD_SIZE] for part in range(parts)], axis=0
    )


def values_of(ref):
    return ref[0:HEAD_SIZE, :]


def queries_of(given_ref, chunk, tokens, grouped):
    parts = given_ref.shape[2] // HEAD_SIZE
    pieces = []
    for j in range(grouped):
        row, column = (1 + j // parts) * tokens, (j % parts) * HEAD_SIZE
        pieces.append(given_ref[chunk, row : row + tokens, column : column + HEAD_SIZE])
    return jnp.concatenate(pieces, axis=0)


def fold(state, distances, pair_refs, own_ref, given_ref, turn, tokens, grouped, scale):
    heads = given_ref.shape[0]
    rows, lanes = heads * tokens, grouped * tokens
    block_index, own = lax.axis_index("blk"), lax.axis_index("head")
    chunk = lax.rem(own - turn + heads, heads)
    place = chunk * tokens + lax.rem(lax.broadcasted_iota(jnp.int32, (1, lanes), 1), tokens)
    own_counts = counts_of(own_ref)
    keys = jnp.concatenate([keys_of(ref) for ref in pair_refs], axis=0)
    values = jnp.concatenate([values_of(ref) for ref in pair_refs], axis=1)
    scores = lax.dot_general(
        keys,
        queries_of(given_ref, chunk, tokens, grouped),
        (((1,), (1,)), ((), ())),
        preferred_element_type=jnp.float32,
    )
    key = lax.broadcasted_iota(jnp.int32, (rows, lanes), 0)
    masked = []
    for which, distance in enumerate(distances):
        begin = jnp.zeros((1, lanes), jnp.float32)
        for own_count, count in zip(own_counts, counts_of(pair_refs[which]), strict=True):
            inside = place.astype(jnp.float32) >= own_count
            begin = jnp.maximum(begin, jnp.where(inside, count, 0.0))
        begin = jnp.where(block_index >= distance, begin.astype(jnp.int32), rows)
        allowed = key >= begin
        if distance == 0:
            allowed = allowed & (key <= place)
        masked.append(jnp.where(allowed, scores[which * rows : (which + 1) * rows], NEG_FILL))
    scores = jnp.concatenate(masked, axis=0)
    top = jnp.max(scores, axis=0, keepdims=True)
    if state is not None:
        old, total, mixed = state
        top = jnp.maximum(old, top)
    weights = jnp.exp2((scores - top) * scale)
    added = jnp.sum(weights, axis=0, keepdims=True)
    moved = jnp.dot(values, weights.astype(jnp.bfloat16), preferred_element_type=jnp.float32)
    if state is None:
        return top, added, moved
    factor = jnp.exp2((old - top) * scale)
    return top, total * factor + added, mixed * factor + moved


def near_kernel(given_ref, *refs, distances, tokens, grouped, scale):
    pair_refs = refs[: len(distances)]
    top_ref, total_ref, mixed_ref = refs[len(distances) :]
    block_index = lax.axis_index("blk")
    levels = sorted(distances) + [lax.axis_size("blk")]
    for level, above in zip(levels[:-1], levels[1:], strict=True):
        taken = [which for which, d in enumerate(distances) if d <= level]

        @pl.when((block_index >= level) & (block_index < above))
        def _(taken=taken):
            for turn in range(given_ref.shape[0]):
                top_ref[turn], total_ref[turn], mixed_ref[turn] = fold(
                    None,
                    [distances[which] for which in taken],
                    [pair_refs[which] for which in taken],
                    pair_refs[0],
                    given_ref,
                    turn,
                    tokens,
                    grouped,
                    scale,
                )


def far_kernel(
    given_ref, own_ref, top_ref, total_ref, mixed_ref, *refs, distances, tokens, grouped, scale
):
    heads = given_ref.shape[0]
    pair_refs = refs[: len(distances)]
    out_refs = refs[len(distances) : len(distances) + heads]
    new_total, new_mixed = refs[len(distances) + heads :]
    block_index = lax.axis_index("blk")

    @pl.when(block_index < min(distances))
    def _():
        new_total[...] = total_ref[...]
        new_mixed[...] = mixed_ref[...]

    levels = sorted(distances) + [lax.axis_size("blk")]
    for level, above in zip(levels[:-1], levels[1:], strict=True):
        taken = [which for which, d in enumerate(distances) if d <= level]

        @pl.when((block_index >= level) & (block_index < above))
        def _(taken=taken):
            for turn in range(heads):
                _, new_total[turn], new_mixed[turn] = fold(
                    (top_ref[turn], total_ref[turn], mixed_ref[turn]),
                    [distances[which] for which in taken],
                    [pair_refs[which] for which in taken],
                    own_ref,
                    given_ref,
                    turn,
                    tokens,
                    grouped,
                    scale,
                )

    for turn in range(heads):
        normed = (new_mixed[turn] * (1.0 / new_total[turn])).astype(jnp.bfloat16).T
        for j in range(grouped):
            out_refs[turn][:, j * HEAD_SIZE : (j + 1) * HEAD_SIZE] = normed[
                j * tokens : (j + 1) * tokens
            ]


def assemble_kernel(*refs, heads):
    pieces, out_ref, semaphores = refs[:heads], refs[heads], refs[heads + 1]
    width = pieces[0].shape[1]
    own = lax.axis_index("head")
    copies = []
    for turn in range(heads):
        start = pl.multiple_of(lax.rem(own + turn, heads) * width, width)
        copies.append(
            pltpu.make_async_copy(
                pieces[turn], out_ref.at[:, pl.ds(start, width)], semaphores.at[turn]
            )
        )
        copies[-1].start()
    for copy in copies:
        copy.wait()


def vmem(count):
    return [pl.BlockSpec(memory_space=pltpu.VMEM)] * count


def cost(tiles, rows, width):
    return pl.CostEstimate(
        flops=4 * tiles * rows * rows * width,
        bytes_accessed=tiles * rows * width * 4,
        transcendentals=tiles * rows * rows,
    )


def call_near(given, pairs, distances, tokens, grouped, scale):
    heads, lanes = given.shape[0], grouped * tokens
    return pl.pallas_call(
        functools.partial(
            near_kernel, distances=distances, tokens=tokens, grouped=grouped, scale=scale
        ),
        out_shape=[
            jax.ShapeDtypeStruct((heads, 1, lanes), jnp.float32),
            jax.ShapeDtypeStruct((heads, 1, lanes), jnp.float32),
            jax.ShapeDtypeStruct((heads, HEAD_SIZE, lanes), jnp.float32),
        ],
        in_specs=vmem(1 + len(distances)),
        out_specs=vmem(3),
        compiler_params=pltpu.CompilerParams(vmem_limit_bytes=16 << 20),
        cost_estimate=cost(len(distances) * heads, heads * tokens, HEAD_SIZE),
        name="attend_near",
    )(given, *pairs)


def call_far(given, own_pairs, state, pairs, distances, tokens, grouped, scale):
    heads, lanes = given.shape[0], grouped * tokens
    return pl.pallas_call(
        functools.partial(
            far_kernel, distances=distances, tokens=tokens, grouped=grouped, scale=scale
        ),
        out_shape=[jax.ShapeDtypeStruct((tokens, grouped * HEAD_SIZE), jnp.bfloat16)] * heads,
        in_specs=vmem(5 + len(distances)),
        out_specs=vmem(heads),
        scratch_shapes=[
            pltpu.VMEM((heads, 1, lanes), jnp.float32),
            pltpu.VMEM((heads, HEAD_SIZE, lanes), jnp.float32),
        ],
        compiler_params=pltpu.CompilerParams(vmem_limit_bytes=16 << 20),
        cost_estimate=cost(len(distances) * heads, heads * tokens, HEAD_SIZE),
        name="attend_far",
    )(given, own_pairs, *state, *pairs)


def per_device(queries, keys_values, segment_ids):
    sections = lax.axis_size("section")
    blocks = lax.axis_size("blk")
    heads = lax.axis_size("head")
    tokens = queries.shape[1]
    rows = tokens * heads
    kv_width = keys_values.shape[2] // heads
    q_width = queries.shape[2] // heads
    grouped = q_width // HEAD_SIZE
    back = min(blocks - 1, -(-LONGEST_SEGMENT // rows))
    scale = math.log2(math.e) / math.sqrt(HEAD_SIZE)

    parts = 1 + q_width // kv_width
    prepared = pl.pallas_call(
        functools.partial(prepare_kernel, heads=heads),
        out_shape=jax.ShapeDtypeStruct(
            (heads, parts * tokens + LABEL_ROWS, kv_width), jnp.bfloat16
        ),
        in_specs=[pl.BlockSpec(memory_space=pltpu.HBM)] * 3,
        out_specs=vmem(1)[0],
        scratch_shapes=[
            pltpu.VMEM((1, tokens), jnp.int32),
            pltpu.VMEM((LABEL_ROWS, kv_width), jnp.float32),
            pltpu.SemaphoreType.DMA((1 + heads * parts,)),
        ],
        compiler_params=pltpu.CompilerParams(vmem_limit_bytes=4 << 20),
        name="prepare",
    )(
        pltpu.with_memory_space_constraint(keys_values[0], pltpu.HBM),
        pltpu.with_memory_space_constraint(segment_ids, pltpu.HBM),
        pltpu.with_memory_space_constraint(queries[0], pltpu.HBM),
    )
    given = lax.all_to_all(prepared, "head", split_axis=0, concat_axis=0, tiled=True)
    own_pairs = pl.pallas_call(
        functools.partial(pack_kernel, tokens=tokens),
        out_shape=jax.ShapeDtypeStruct((2 * HEAD_SIZE + LABEL_ROWS, rows), jnp.bfloat16),
        in_specs=vmem(1),
        out_specs=vmem(1)[0],
        scratch_shapes=[pltpu.VMEM((LABEL_ROWS, kv_width), jnp.float32)],
        compiler_params=pltpu.CompilerParams(vmem_limit_bytes=4 << 20),
        name="pack",
    )(given)
    pairs = {0: own_pairs}
    for d, held in SENT.items():
        if d <= back:
            route = [(i, i + d - held) for i in range(held, blocks - d + held)]
            pairs[d] = lax.ppermute(pairs[held], "blk", route)
    near = tuple(d for d in NEAR if d <= back)
    far = tuple(d for d in FAR if d <= back)
    state = call_near(given, [pairs[d] for d in near], near, tokens, grouped, scale)
    attended = call_far(
        given, own_pairs, state, [pairs[d] for d in far], far, tokens, grouped, scale
    )

    def index(section, block, head):
        return ((section % sections) * blocks + block) * heads + head % heads

    received = [None] * heads
    for turn in range(heads):
        route = [
            (index(s, b, h), index(s + 1, b, h - turn))
            for s in range(sections)
            for b in range(blocks)
            for h in range(heads)
        ]
        received[turn] = lax.ppermute(attended[turn], ("section", "blk", "head"), route)
    result = pl.pallas_call(
        functools.partial(assemble_kernel, heads=heads),
        out_shape=jax.ShapeDtypeStruct(queries.shape[1:], jnp.bfloat16),
        in_specs=vmem(heads),
        out_specs=pl.BlockSpec(memory_space=pl.ANY),
        scratch_shapes=[pltpu.SemaphoreType.DMA((heads,))],
        compiler_params=pltpu.CompilerParams(vmem_limit_bytes=4 << 20),
        name="assemble",
    )(*received)
    return result[None]


def solution(mesh):
    return jax.shard_map(
        per_device,
        mesh=mesh,
        in_specs=(
            P("section", ("blk", "head"), None),
            P("section", ("blk", "head"), None),
            P("section", ("blk", "head")),
        ),
        out_specs=P("section", ("blk", "head"), None),
        check_vma=False,
    )
```
